512 devices in a mesh: row: 16 (over z, core), col: 32 (over y, x).
Axes of the slice: x: 4, y: 8, z: 8, core: 2. Of those that a mesh axis runs over, the one named last changes fastest.
Arguments:
- embeddings: bfloat16 [2048, 512], P('row'), may hold values from -6 to 6
- row_weight: bfloat16 [512, 32], replicated, may hold values from -0.25 to 0.25
- col_weight: bfloat16 [512, 32], replicated, may hold values from -0.25 to 0.25
- conv_weights: bfloat16 [3, 32, 32, 3, 3], replicated, may hold values from -0.5 to 0.5
- conv_bias: float32 [3, 32], replicated, may hold values from -3 to 3
- head_weight: bfloat16 [32], replicated, may hold values from -1 to 1
Outputs:
- contact_map: float32 [2048, 2048], P('row', 'col')
The draws below stay inside these ranges and needn't reach their ends.
All inputs are finite; a program needn't handle non-finite values.
Results may differ from the reference program's by a relative error of at most 0.023.
Values may be sent and summed in bfloat16 or wider, within the bound.
A program may use at most 64 MiB of HBM per device.

```python
import jax
import jax.numpy as jnp
from jax import lax

EMB = 512
PCH = 32
N_BINS = 2048
N_ROW = 16


def block_scale(stream_key, shape, cuts, least, largest):
    loudness = 1.0
    for axis_at, blocks in cuts:
        draws = jax.random.uniform(jax.random.fold_in(jax.random.fold_in(stream_key, 6), axis_at), (blocks,), jnp.float32, least / len(cuts), largest / len(cuts))
        loudness = loudness * jnp.repeat(jnp.exp(draws), shape[axis_at] // blocks).reshape((-1,) + (1,) * (len(shape) - 1 - axis_at))
    return loudness


def bell_draw(key, shape, width, most, split=(), kind=jnp.bfloat16):
    array = width * jax.random.normal(key, shape, jnp.float32)
    if split:
        array = array * block_scale(key, shape, split, -0.22, 0.18)
    return jnp.clip(array, -most, most).astype(kind)


def setup_inputs(seed: int = 0) -> dict:
    keys = jax.random.split(jax.random.key(seed), 7)
    embeddings = bell_draw(keys[0], (N_BINS, EMB), 1.0, 6.0, ((0, 16),))
    row_weight = bell_draw(keys[1], (EMB, PCH), EMB ** -0.5, 0.25)
    col_weight = bell_draw(keys[2], (EMB, PCH), EMB ** -0.5, 0.25)
    conv_weights = bell_draw(keys[3], (3, PCH, PCH, 3, 3), (9 * PCH // 2) ** -0.5, 0.5)
    conv_bias = bell_draw(keys[4], (3, PCH), 0.5, 3.0, (), jnp.float32)
    head_weight = bell_draw(keys[5], (PCH,), PCH ** -0.5, 1.0)
    return dict(embeddings=embeddings, row_weight=row_weight, col_weight=col_weight, conv_weights=conv_weights, conv_bias=conv_bias, head_weight=head_weight)


def dilated_level(values, weight, level_bias, dilation):
    summed = lax.conv_general_dilated(values.astype(jnp.float32)[None], weight.astype(jnp.float32), (1, 1), "VALID", rhs_dilation=(dilation, dilation), dimension_numbers=("NCHW", "OIHW", "NCHW"), precision=lax.Precision.HIGHEST)[0]
    return jax.nn.relu(summed + level_bias[:, None, None]).astype(jnp.bfloat16)


def clear_outside(values, row_inside, col_inside):
    inside = row_inside[:, None] & col_inside[None, :]
    return jnp.where(inside[None], values, jnp.zeros((), values.dtype))


def reference(embeddings, row_weight, col_weight, conv_weights, conv_bias, head_weight):
    total_bins = embeddings.shape[0]
    block_rows = total_bins // N_ROW
    margin = 7
    first_proj = jnp.dot(embeddings, row_weight, preferred_element_type=jnp.float32).astype(jnp.bfloat16)
    second_proj = jnp.dot(embeddings, col_weight, preferred_element_type=jnp.float32).astype(jnp.bfloat16)
    row_wide = jnp.pad(first_proj, ((margin, margin), (0, 0)))
    col_wide = jnp.pad(second_proj, ((margin, margin), (0, 0)))
    col_at = jnp.arange(total_bins + 2 * margin, dtype=jnp.int32) - margin
    col_inside = (col_at >= 0) & (col_at < total_bins)

    def one_block(block_index):
        first = (block_index * block_rows).astype(jnp.int32)
        rows_part = lax.dynamic_slice_in_dim(row_wide, first, block_rows + 2 * margin, 0)
        row_at = first - margin + jnp.arange(block_rows + 2 * margin, dtype=jnp.int32)
        row_inside = (row_at >= 0) & (row_at < total_bins)
        current = (rows_part.T.astype(jnp.float32)[:, :, None] + col_wide.T.astype(jnp.float32)[:, None, :]).astype(jnp.bfloat16)
        current = clear_outside(current, row_inside, col_inside)
        remaining = margin
        for level_number, dilation in enumerate((1, 2, 4)):
            current = dilated_level(current, conv_weights[level_number], conv_bias[level_number], dilation)
            remaining = remaining - dilation
            trimmed = margin - remaining
            current = clear_outside(current, row_inside[trimmed:row_inside.shape[0] - trimmed], col_inside[trimmed:col_inside.shape[0] - trimmed])
        return jnp.einsum("c,crj->rj", head_weight.astype(jnp.float32), current.astype(jnp.float32), precision=lax.Precision.HIGHEST)

    blocks = lax.map(one_block, jnp.arange(N_ROW, dtype=jnp.int32))
    return blocks.reshape(total_bins, total_bins)
```

```python
import jax
import jax.numpy as jnp
from jax import lax
from jax.experimental import pallas as pl
from jax.experimental.pallas import tpu as pltpu
from jax.sharding import PartitionSpec as P

CH = 32
ROWS = 128
COLS = 64
LANES = 128
HALO = 7
TALL = ROWS + 2 * HALO
GROUP = 6
SPAN = GROUP + 2
SIDE = 32
DILATIONS = (1, 2, 4)


def exchange_kernel(emb_ref, row_w_ref, col_w_ref, out_ref, own, land, send_sem, recv_sem):
    n = lax.axis_size("row")
    m = lax.axis_size("col")
    r = lax.axis_index("row")
    c = lax.axis_index("col")
    half = c % 2
    owner = c // 2
    side = owner - 1 + 2 * half
    has_side = jnp.logical_and(side >= 0, side < n)
    is_owner = r == owner
    is_side = r == side
    barrier = pltpu.get_barrier_semaphore()

    def greet(row):
        pl.semaphore_signal(
            barrier, inc=1, device_id=(row, c), device_id_type=pl.DeviceIdType.MESH
        )

    pl.when(r > 0)(lambda: greet(r - 1))
    pl.when(r < n - 1)(lambda: greet(r + 1))
    pl.when(jnp.logical_not(is_owner))(lambda: greet(owner))
    pl.when(jnp.logical_and(has_side, jnp.logical_not(is_side)))(lambda: greet(side))

    for at, w_ref in enumerate((row_w_ref, col_w_ref)):
        own[at] = lax.dot_general(
            w_ref[...], emb_ref[...], (((0,), (1,)), ((), ())), preferred_element_type=jnp.float32
        ).astype(jnp.bfloat16)

    expected = (
        jnp.where(r > 0, 1, 0)
        + jnp.where(r < n - 1, 1, 0)
        + jnp.where(is_owner, n - 1, 0)
        + jnp.where(is_side, n - 1, 0)
    )
    pl.semaphore_wait(barrier, expected)

    def copy(source, slot, row, sem):
        return pltpu.make_async_remote_copy(
            src_ref=own.at[source],
            dst_ref=land.at[slot],
            send_sem=send_sem.at[sem],
            recv_sem=recv_sem.at[slot],
            device_id=(row, c),
            device_id_type=pl.DeviceIdType.MESH,
        )

    def broadcast(slot):
        order = sorted(range(1, n), key=lambda k: -min(k, n - k))
        for k in order:
            copy(1, slot, (r + k) % n, 1 + k).start()

    def finish():
        for k in range(1, n):
            copy(1, 2, (r + k) % n, 1 + k).wait_send()

    pl.when(is_owner)(lambda: broadcast(2))
    pl.when(is_side)(lambda: broadcast(3))
    pl.when(r > 0)(lambda: copy(0, 1, r - 1, 0).start())
    pl.when(r < n - 1)(lambda: copy(0, 0, r + 1, 1).start())

    def fill(slot, value):
        land[slot] = value

    blank = jnp.zeros((CH, LANES), jnp.bfloat16)
    pl.when(is_owner)(lambda: fill(2, own[1]))
    pl.when(is_side)(lambda: fill(3, own[1]))
    pl.when(jnp.logical_not(has_side))(lambda: fill(3, blank))
    pl.when(r == 0)(lambda: fill(0, blank))
    pl.when(r == n - 1)(lambda: fill(1, blank))

    pl.when(r > 0)(lambda: copy(0, 0, r - 1, 0).wait_recv())
    pl.when(r < n - 1)(lambda: copy(0, 1, r + 1, 1).wait_recv())
    pl.when(jnp.logical_not(is_owner))(lambda: copy(1, 2, owner, 2).wait_recv())
    pl.when(jnp.logical_and(has_side, jnp.logical_not(is_side)))(
        lambda: copy(1, 3, side, 2).wait_recv()
    )
    for slot in range(4):
        out_ref[slot] = land[slot]
    out_ref[4] = own[0]
    pl.when(r > 0)(lambda: copy(0, 1, r - 1, 0).wait_send())
    pl.when(r < n - 1)(lambda: copy(0, 0, r + 1, 1).wait_send())
    pl.when(jnp.logical_or(is_owner, is_side))(finish)


def starts(level):
    dilation = DILATIONS[level]
    reach = sum(DILATIONS[: level + 1])
    first, last = reach, TALL - reach
    found = []
    for phase in range(dilation):
        rows = list(range(first + phase, last, dilation))
        at = 0
        while at < len(rows):
            at = min(at, len(rows) - GROUP)
            found.append(rows[at])
            at += GROUP
    return found


def map_kernel(feat_ref, w_ref, bias_ref, head_ref, out_ref, xa, xb, toep, gathered):
    n = lax.axis_size("row")
    m = lax.axis_size("col")
    r = lax.axis_index("row")
    c = lax.axis_index("col")
    half = c % 2
    f32, bf16 = jnp.float32, jnp.bfloat16

    for at in range(9):
        base = w_ref[at].astype(f32)
        for p in range(GROUP):
            moved = base if p == 0 else pltpu.roll(base, CH * p, 1)
            toep[at, p * CH : (p + 1) * CH, :] = moved.astype(bf16)

    lane = lax.broadcasted_iota(jnp.int32, (CH, LANES), 1)
    column = lane + (c * COLS - SIDE)
    inside = jnp.logical_and(column >= 0, column < m * COLS)
    keep = jnp.where(inside, 1.0, 0.0).astype(bf16)

    col_own = feat_ref[2].astype(f32)
    col_side = feat_ref[3].astype(f32)
    low = jnp.where(lane >= SIDE, pltpu.roll(col_own, SIDE, 1), pltpu.roll(col_side, SIDE, 1))
    high = jnp.where(
        lane < LANES - SIDE,
        pltpu.roll(col_own, LANES - SIDE, 1),
        pltpu.roll(col_side, LANES - SIDE, 1),
    )
    cols = jnp.where(half == 0, low, high)

    def put(ref, row, value, dilation):
        ref[1, row] = value
        wide = value.astype(f32)
        ref[0, row] = pltpu.roll(wide, dilation, 1).astype(bf16)
        ref[2, row] = pltpu.roll(wide, LANES - dilation, 1).astype(bf16)

    def clear(ref, level):
        reach = sum(DILATIONS[:level])

        def top():
            for row in range(reach, HALO):
                for tap in range(3):
                    ref[tap, row] = jnp.zeros((CH, LANES), bf16)

        def bottom():
            for row in range(TALL - HALO, TALL - reach):
                for tap in range(3):
                    ref[tap, row] = jnp.zeros((CH, LANES), bf16)

        pl.when(r == 0)(top)
        pl.when(r == n - 1)(bottom)

    keep_wide = keep.astype(f32)
    shifted = [
        pltpu.roll(cols, DILATIONS[0], 1),
        cols,
        pltpu.roll(cols, LANES - DILATIONS[0], 1),
    ]
    kept = [
        pltpu.roll(keep_wide, DILATIONS[0], 1).astype(bf16),
        keep,
        pltpu.roll(keep_wide, LANES - DILATIONS[0], 1).astype(bf16),
    ]
    for slot, lanes, at in (
        (0, range(LANES - HALO, LANES), 0),
        (4, range(LANES), HALO),
        (1, range(HALO), HALO + ROWS),
    ):
        slab = feat_ref[slot].astype(f32)
        for row, where in enumerate(lanes):
            one = jnp.broadcast_to(slab[:, where : where + 1], (CH, LANES))
            for tap in range(3):
                xa[tap, at + row] = (one + shifted[tap]).astype(bf16) * kept[tap]
    clear(xa, 0)

    diagonal = lax.broadcasted_iota(jnp.int32, (CH, CH), 0) == lax.broadcasted_iota(
        jnp.int32, (CH, CH), 1
    )

    def level_bias(level):
        spread = jnp.where(diagonal, bias_ref[level : level + 1, :], 0.0)
        return jnp.broadcast_to(jnp.sum(spread, axis=1, keepdims=True), (CH, LANES))

    tile_from = lax.broadcasted_iota(jnp.int32, (CH, GROUP * CH), 0)
    tile_to = lax.broadcasted_iota(jnp.int32, (CH, GROUP * CH), 1)
    tiler = jnp.where(tile_to % CH == tile_from, 1.0, 0.0).astype(bf16)
    head_rows = jnp.broadcast_to(head_ref[...].astype(f32), (8, CH)).astype(bf16)
    tiled = jnp.dot(head_rows, tiler, preferred_element_type=f32)
    line = lax.broadcasted_iota(jnp.int32, (8, GROUP * CH), 0)
    spot = lax.broadcasted_iota(jnp.int32, (8, GROUP * CH), 1)
    head = jnp.where(spot // CH == line, tiled, 0.0).astype(bf16)

    def window(ref, tap, start, dilation):
        return jnp.concatenate(
            [ref[tap, start + dilation * (q - 1)] for q in range(SPAN)], axis=0
        )

    refs = (xa, xb, xa)
    for level, dilation in enumerate(DILATIONS):
        source = refs[level]
        bias = level_bias(level)
        bias = jnp.concatenate([bias, bias], axis=1)
        bias = jnp.concatenate([bias] * GROUP, axis=0)
        begun = starts(level)
        for left, right in zip(begun[0::2], begun[1::2]):
            total = None
            for tap in range(3):
                seen = jnp.concatenate(
                    [window(source, tap, left, dilation), window(source, tap, right, dilation)],
                    axis=1,
                )
                part = jnp.dot(toep[level * 3 + tap], seen, preferred_element_type=f32)
                total = part if total is None else total + part
            value = jnp.maximum(total + bias, 0.0).astype(bf16)
            if level < 2:
                for part, start in enumerate((left, right)):
                    for p in range(GROUP):
                        piece = value[p * CH : (p + 1) * CH, part * LANES : (part + 1) * LANES]
                        put(refs[level + 1], start + dilation * p, piece * keep, DILATIONS[level + 1])
            else:
                line_out = jnp.dot(head, value, preferred_element_type=f32)
                for part, start in enumerate((left, right)):
                    for p in range(GROUP):
                        row = start + dilation * p - HALO
                        gathered[row : row + 1, :] = line_out[
                            p : p + 1, part * LANES : (part + 1) * LANES
                        ]
        if level < 2:
            clear(refs[level + 1], level + 1)
    out_ref[...] = pltpu.roll(gathered[...], LANES - SIDE, 1)[:, :COLS]


def body(embeddings, row_weight, col_weight, conv_weights, conv_bias, head_weight):
    n = lax.axis_size("row")
    vmem = pl.BlockSpec(memory_space=pltpu.VMEM)
    feats = pl.pallas_call(
        exchange_kernel,
        out_shape=jax.ShapeDtypeStruct((5, CH, LANES), jnp.bfloat16),
        in_specs=[vmem] * 3,
        out_specs=vmem,
        scratch_shapes=[
            pltpu.VMEM((2, CH, LANES), jnp.bfloat16),
            pltpu.VMEM((4, CH, LANES), jnp.bfloat16),
            pltpu.SemaphoreType.DMA((n + 1,)),
            pltpu.SemaphoreType.DMA((4,)),
        ],
        compiler_params=pltpu.CompilerParams(collective_id=0, has_side_effects=True),
        name="exchange",
    )(embeddings, row_weight, col_weight)
    base = conv_weights.transpose(0, 4, 1, 3, 2).reshape(9, CH, 3 * CH)
    base = jnp.pad(base, ((0, 0), (0, 0), (0, SPAN * CH - 3 * CH)))
    return pl.pallas_call(
        map_kernel,
        out_shape=jax.ShapeDtypeStruct((ROWS, COLS), jnp.float32),
        in_specs=[vmem] * 4,
        out_specs=vmem,
        scratch_shapes=[
            pltpu.VMEM((3, TALL, CH, LANES), jnp.bfloat16),
            pltpu.VMEM((3, TALL, CH, LANES), jnp.bfloat16),
            pltpu.VMEM((9, GROUP * CH, SPAN * CH), jnp.bfloat16),
            pltpu.VMEM((ROWS, LANES), jnp.float32),
        ],
        name="contact",
    )(feats, base, conv_bias, head_weight.reshape(1, CH))


def solution(mesh):
    return jax.shard_map(
        body,
        mesh=mesh,
        in_specs=(P("row", None), P(), P(), P(), P(), P()),
        out_specs=P("row", "col"),
        check_vma=False,
    )
```

```python
import jax
import jax.numpy as jnp
from jax import lax
from jax.experimental import pallas as pl
from jax.experimental.pallas import tpu as pltpu
from jax.sharding import PartitionSpec as P

CH = 32
ROWS = 128
COLS = 64
LANES = 128
HALO = 7
TALL = ROWS + 2 * HALO
GROUP = 6
SPAN = GROUP + 2
SIDE = 32
DILATIONS = (1, 2, 4)


def exchange_kernel(
    emb_hbm,
    row_w_hbm,
    col_w_hbm,
    w_hbm,
    out_ref,
    toep,
    emb_ref,
    proj_ref,
    w_ref,
    own,
    land,
    load_sem,
    send_sem,
    recv_sem,
):
    loads = [
        pltpu.make_async_copy(source, target, load_sem.at[at])
        for at, (source, target) in enumerate(
            (
                (emb_hbm, emb_ref),
                (row_w_hbm, proj_ref.at[0]),
                (col_w_hbm, proj_ref.at[1]),
                (w_hbm, w_ref),
            )
        )
    ]
    for load in loads:
        load.start()

    n = lax.axis_size("row")
    m = lax.axis_size("col")
    r = lax.axis_index("row")
    c = lax.axis_index("col")
    half = c % 2
    owner = c // 2
    side = owner - 1 + 2 * half
    has_side = jnp.logical_and(side >= 0, side < n)
    is_owner = r == owner
    is_side = r == side
    barrier = pltpu.get_barrier_semaphore()

    def greet(row):
        pl.semaphore_signal(
            barrier, inc=1, device_id=(row, c), device_id_type=pl.DeviceIdType.MESH
        )

    pl.when(r > 0)(lambda: greet(r - 1))
    pl.when(r < n - 1)(lambda: greet(r + 1))
    pl.when(jnp.logical_not(is_owner))(lambda: greet(owner))
    pl.when(jnp.logical_and(has_side, jnp.logical_not(is_side)))(lambda: greet(side))

    for load in loads[:3]:
        load.wait()
    projected = lax.dot_general(
        jnp.concatenate([proj_ref[0], proj_ref[1]], axis=0),
        emb_ref[...],
        (((1,), (1,)), ((), ())),
        preferred_element_type=jnp.float32,
    ).astype(jnp.bfloat16)
    own[0] = projected[:CH]
    own[1] = projected[CH:]

    expected = (
        jnp.where(r > 0, 1, 0)
        + jnp.where(r < n - 1, 1, 0)
        + jnp.where(is_owner, n - 1, 0)
        + jnp.where(is_side, n - 1, 0)
    )
    pl.semaphore_wait(barrier, expected)

    def copy(source, slot, row, sem):
        return pltpu.make_async_remote_copy(
            src_ref=own.at[source],
            dst_ref=land.at[slot],
            send_sem=send_sem.at[sem],
            recv_sem=recv_sem.at[slot],
            device_id=(row, c),
            device_id_type=pl.DeviceIdType.MESH,
        )

    def broadcast(slot):
        order = sorted(range(1, n), key=lambda k: -min(k, n - k))
        for k in order:
            copy(1, slot, (r + k) % n, 1 + k).start()

    def finish():
        for k in range(1, n):
            copy(1, 2, (r + k) % n, 1 + k).wait_send()

    pl.when(is_owner)(lambda: broadcast(2))
    pl.when(is_side)(lambda: broadcast(3))
    pl.when(r > 0)(lambda: copy(0, 1, r - 1, 0).start())
    pl.when(r < n - 1)(lambda: copy(0, 0, r + 1, 1).start())

    def fill(slot, value):
        land[slot] = value

    blank = jnp.zeros((CH, LANES), jnp.bfloat16)
    pl.when(is_owner)(lambda: fill(2, own[1]))
    pl.when(is_side)(lambda: fill(3, own[1]))
    pl.when(jnp.logical_not(has_side))(lambda: fill(3, blank))
    pl.when(r == 0)(lambda: fill(0, blank))
    pl.when(r == n - 1)(lambda: fill(1, blank))

    toep[...] = jnp.zeros_like(toep)
    loads[3].wait()
    for level in range(3):
        for b in range(3):
            for a in range(3):
                tap = w_ref[level, a, b]
                for p in range(GROUP):
                    at = CH * (p + a)
                    toep[level * 3 + b, p * CH : (p + 1) * CH, at : at + CH] = tap

    pl.when(r > 0)(lambda: copy(0, 0, r - 1, 0).wait_recv())
    pl.when(r < n - 1)(lambda: copy(0, 1, r + 1, 1).wait_recv())
    pl.when(jnp.logical_not(is_owner))(lambda: copy(1, 2, owner, 2).wait_recv())
    pl.when(jnp.logical_and(has_side, jnp.logical_not(is_side)))(
        lambda: copy(1, 3, side, 2).wait_recv()
    )
    for slot in range(4):
        out_ref[slot] = land[slot]
    out_ref[4] = own[0]
    pl.when(r > 0)(lambda: copy(0, 1, r - 1, 0).wait_send())
    pl.when(r < n - 1)(lambda: copy(0, 0, r + 1, 1).wait_send())
    pl.when(jnp.logical_or(is_owner, is_side))(finish)


def starts(level):
    dilation = DILATIONS[level]
    reach = sum(DILATIONS[: level + 1])
    first, last = reach, TALL - reach
    found = []
    for phase in range(dilation):
        rows = list(range(first + phase, last, dilation))
        at = 0
        while at < len(rows):
            at = min(at, len(rows) - GROUP)
            found.append(rows[at])
            at += GROUP
    return found


def map_kernel(feat_ref, toep, bias_ref, head_ref, out_ref, xa, xb, gathered):
    n = lax.axis_size("row")
    m = lax.axis_size("col")
    r = lax.axis_index("row")
    c = lax.axis_index("col")
    half = c % 2
    f32, bf16 = jnp.float32, jnp.bfloat16

    lane = lax.broadcasted_iota(jnp.int32, (CH, LANES), 1)
    column = lane + (c * COLS - SIDE)
    inside = jnp.logical_and(column >= 0, column < m * COLS)
    keep = jnp.where(inside, 1.0, 0.0).astype(bf16)

    col_own = feat_ref[2].astype(f32)
    col_side = feat_ref[3].astype(f32)
    low = jnp.where(lane >= SIDE, pltpu.roll(col_own, SIDE, 1), pltpu.roll(col_side, SIDE, 1))
    high = jnp.where(
        lane < LANES - SIDE,
        pltpu.roll(col_own, LANES - SIDE, 1),
        pltpu.roll(col_side, LANES - SIDE, 1),
    )
    cols = jnp.where(half == 0, low, high)

    def put(ref, row, value, dilation):
        ref[1, row] = value
        wide = value.astype(f32)
        ref[0, row] = pltpu.roll(wide, dilation, 1).astype(bf16)
        ref[2, row] = pltpu.roll(wide, LANES - dilation, 1).astype(bf16)

    def clear(ref, level):
        reach = sum(DILATIONS[:level])

        def top():
            for row in range(reach, HALO):
                for tap in range(3):
                    ref[tap, row] = jnp.zeros((CH, LANES), bf16)

        def bottom():
            for row in range(TALL - HALO, TALL - reach):
                for tap in range(3):
                    ref[tap, row] = jnp.zeros((CH, LANES), bf16)

        pl.when(r == 0)(top)
        pl.when(r == n - 1)(bottom)

    keep_wide = keep.astype(f32)
    shifted = [
        pltpu.roll(cols, DILATIONS[0], 1),
        cols,
        pltpu.roll(cols, LANES - DILATIONS[0], 1),
    ]
    kept = [
        pltpu.roll(keep_wide, DILATIONS[0], 1).astype(bf16),
        keep,
        pltpu.roll(keep_wide, LANES - DILATIONS[0], 1).astype(bf16),
    ]
    for slot, lanes, at in (
        (0, range(LANES - HALO, LANES), 0),
        (4, range(LANES), HALO),
        (1, range(HALO), HALO + ROWS),
    ):
        slab = feat_ref[slot].astype(f32)
        for row, where in enumerate(lanes):
            one = jnp.broadcast_to(slab[:, where : where + 1], (CH, LANES))
            for tap in range(3):
                xa[tap, at + row] = (one + shifted[tap]).astype(bf16) * kept[tap]
    clear(xa, 0)

    diagonal = lax.broadcasted_iota(jnp.int32, (CH, CH), 0) == lax.broadcasted_iota(
        jnp.int32, (CH, CH), 1
    )

    def level_bias(level):
        spread = jnp.where(diagonal, bias_ref[level : level + 1, :], 0.0)
        return jnp.broadcast_to(jnp.sum(spread, axis=1, keepdims=True), (CH, LANES))

    tile_from = lax.broadcasted_iota(jnp.int32, (CH, GROUP * CH), 0)
    tile_to = lax.broadcasted_iota(jnp.int32, (CH, GROUP * CH), 1)
    tiler = jnp.where(tile_to % CH == tile_from, 1.0, 0.0).astype(bf16)
    head_rows = jnp.broadcast_to(head_ref[...].astype(f32), (8, CH)).astype(bf16)
    tiled = jnp.dot(head_rows, tiler, preferred_element_type=f32)
    line = lax.broadcasted_iota(jnp.int32, (8, GROUP * CH), 0)
    spot = lax.broadcasted_iota(jnp.int32, (8, GROUP * CH), 1)
    head = jnp.where(spot // CH == line, tiled, 0.0).astype(bf16)

    def window(ref, tap, start, dilation):
        return jnp.concatenate(
            [ref[tap, start + dilation * (q - 1)] for q in range(SPAN)], axis=0
        )

    refs = (xa, xb, xa)
    for level, dilation in enumerate(DILATIONS):
        source = refs[level]
        bias = level_bias(level)
        bias = jnp.concatenate([bias, bias], axis=1)
        bias = jnp.concatenate([bias] * GROUP, axis=0)
        begun = starts(level)
        for left, right in zip(begun[0::2], begun[1::2]):
            total = None
            for tap in range(3):
                seen = jnp.concatenate(
                    [window(source, tap, left, dilation), window(source, tap, right, dilation)],
                    axis=1,
                )
                part = jnp.dot(toep[level * 3 + tap], seen, preferred_element_type=f32)
                total = part if total is None else total + part
            value = jnp.maximum(total + bias, 0.0).astype(bf16)
            if level < 2:
                for part, start in enumerate((left, right)):
                    for p in range(GROUP):
                        piece = value[p * CH : (p + 1) * CH, part * LANES : (part + 1) * LANES]
                        put(refs[level + 1], start + dilation * p, piece * keep, DILATIONS[level + 1])
            else:
                line_out = jnp.dot(head, value, preferred_element_type=f32)
                for part, start in enumerate((left, right)):
                    for p in range(GROUP):
                        row = start + dilation * p - HALO
                        gathered[row : row + 1, :] = line_out[
                            p : p + 1, part * LANES : (part + 1) * LANES
                        ]
        if level < 2:
            clear(refs[level + 1], level + 1)
    out_ref[...] = gathered[...].T[SIDE : SIDE + COLS]


def body(embeddings, row_weight, col_weight, conv_weights, conv_bias, head_weight):
    n = lax.axis_size("row")
    vmem = pl.BlockSpec(memory_space=pltpu.VMEM)
    feats, banded = pl.pallas_call(
        exchange_kernel,
        out_shape=(
            jax.ShapeDtypeStruct((5, CH, LANES), jnp.bfloat16),
            jax.ShapeDtypeStruct((9, GROUP * CH, SPAN * CH), jnp.bfloat16),
        ),
        in_specs=[pl.BlockSpec(memory_space=pltpu.HBM)] * 4,
        out_specs=(vmem, vmem),
        scratch_shapes=[
            pltpu.VMEM(embeddings.shape, jnp.bfloat16),
            pltpu.VMEM((2, CH, embeddings.shape[1]), jnp.bfloat16),
            pltpu.VMEM((3, 3, 3, CH, CH), jnp.bfloat16),
            pltpu.VMEM((2, CH, LANES), jnp.bfloat16),
            pltpu.VMEM((4, CH, LANES), jnp.bfloat16),
            pltpu.SemaphoreType.DMA((4,)),
            pltpu.SemaphoreType.DMA((n + 1,)),
            pltpu.SemaphoreType.DMA((4,)),
        ],
        compiler_params=pltpu.CompilerParams(
            collective_id=0, has_side_effects=True, vmem_limit_bytes=16 * 2**20
        ),
        name="exchange",
    )(embeddings, row_weight.T, col_weight.T, conv_weights.transpose(0, 3, 4, 1, 2))
    contact = pl.pallas_call(
        map_kernel,
        out_shape=jax.ShapeDtypeStruct((COLS, ROWS), jnp.float32),
        in_specs=[vmem] * 4,
        out_specs=vmem,
        scratch_shapes=[
            pltpu.VMEM((3, TALL, CH, LANES), jnp.bfloat16),
            pltpu.VMEM((3, TALL, CH, LANES), jnp.bfloat16),
            pltpu.VMEM((ROWS, LANES), jnp.float32),
        ],
        compiler_params=pltpu.CompilerParams(vmem_limit_bytes=24 * 2**20),
        name="contact",
    )(feats, banded, conv_bias, head_weight.reshape(1, CH))
    return contact.T


def solution(mesh):
    return jax.shard_map(
        body,
        mesh=mesh,
        in_specs=(P("row", None), P(), P(), P(), P(), P()),
        out_specs=P("row", "col"),
        check_vma=False,
    )
```

```python
import jax
import jax.numpy as jnp
from jax import lax
from jax.experimental import pallas as pl
from jax.experimental.pallas import tpu as pltpu
from jax.sharding import PartitionSpec as P

CH = 32
ROWS = 128
COLS = 64
LANES = 128
HALO = 7
TALL = ROWS + 2 * HALO
GROUP = 6
SPAN = GROUP + 2
SIDE = 32
DILATIONS = (1, 2, 4)


def starts(level):
    dilation = DILATIONS[level]
    reach = sum(DILATIONS[: level + 1])
    first, last = reach, TALL - reach
    found = []
    for phase in range(dilation):
        rows = list(range(first + phase, last, dilation))
        at = 0
        while at < len(rows):
            at = min(at, len(rows) - GROUP)
            found.append(rows[at])
            at += GROUP
    return found


def contact_kernel(
    emb_hbm,
    row_w_hbm,
    col_w_hbm,
    w_hbm,
    bias_hbm,
    head_hbm,
    out_ref,
    emb_ref,
    proj_ref,
    w_ref,
    bias_ref,
    head_ref,
    own,
    land,
    toep,
    xa,
    xb,
    last,
    gathered,
    load_sem,
    send_sem,
    recv_sem,
):
    loads = [
        pltpu.make_async_copy(source, target, load_sem.at[at])
        for at, (source, target) in enumerate(
            (
                (emb_hbm, emb_ref),
                (row_w_hbm, proj_ref.at[0]),
                (col_w_hbm, proj_ref.at[1]),
                (w_hbm, w_ref),
                (bias_hbm, bias_ref),
                (head_hbm, head_ref),
            )
        )
    ]
    for load in loads:
        load.start()

    n = lax.axis_size("row")
    m = lax.axis_size("col")
    r = lax.axis_index("row")
    c = lax.axis_index("col")
    half = c % 2
    owner = c // 2
    side = owner - 1 + 2 * half
    has_side = jnp.logical_and(side >= 0, side < n)
    is_owner = r == owner
    is_side = r == side
    barrier = pltpu.get_barrier_semaphore()

    def greet(row):
        pl.semaphore_signal(
            barrier, inc=1, device_id=(row, c), device_id_type=pl.DeviceIdType.MESH
        )

    pl.when(r > 0)(lambda: greet(r - 1))
    pl.when(r < n - 1)(lambda: greet(r + 1))
    pl.when(jnp.logical_not(is_owner))(lambda: greet(owner))
    pl.when(jnp.logical_and(has_side, jnp.logical_not(is_side)))(lambda: greet(side))

    for load in loads[:3]:
        load.wait()
    projected = lax.dot_general(
        jnp.concatenate([proj_ref[0], proj_ref[1]], axis=0),
        emb_ref[...],
        (((1,), (1,)), ((), ())),
        preferred_element_type=jnp.float32,
    ).astype(jnp.bfloat16)
    own[0] = projected[:CH]
    own[1] = projected[CH:]

    expected = (
        jnp.where(r > 0, 1, 0)
        + jnp.where(r < n - 1, 1, 0)
        + jnp.where(is_owner, n - 1, 0)
        + jnp.where(is_side, n - 1, 0)
    )
    pl.semaphore_wait(barrier, expected)

    def copy(source, slot, row, sem):
        return pltpu.make_async_remote_copy(
            src_ref=own.at[source],
            dst_ref=land.at[slot],
            send_sem=send_sem.at[sem],
            recv_sem=recv_sem.at[slot],
            device_id=(row, c),
            device_id_type=pl.DeviceIdType.MESH,
        )

    def broadcast(slot):
        order = sorted(range(1, n), key=lambda k: -min(k, n - k))
        for k in order:
            copy(1, slot, (r + k) % n, 1 + k).start()

    def finish():
        for k in range(1, n):
            copy(1, 2, (r + k) % n, 1 + k).wait_send()

    pl.when(is_owner)(lambda: broadcast(2))
    pl.when(is_side)(lambda: broadcast(3))
    pl.when(r > 0)(lambda: copy(0, 1, r - 1, 0).start())
    pl.when(r < n - 1)(lambda: copy(0, 0, r + 1, 1).start())

    def fill(slot, value):
        land[slot] = value

    blank = jnp.zeros((CH, LANES), jnp.bfloat16)
    pl.when(is_owner)(lambda: fill(2, own[1]))
    pl.when(is_side)(lambda: fill(3, own[1]))
    pl.when(jnp.logical_not(has_side))(lambda: fill(3, blank))
    pl.when(r == 0)(lambda: fill(0, blank))
    pl.when(r == n - 1)(lambda: fill(1, blank))

    toep[...] = jnp.zeros_like(toep)
    for load in loads[3:]:
        load.wait()
    for level in range(3):
        for b in range(3):
            for a in range(3):
                tap = w_ref[level, a, b]
                for p in range(GROUP):
                    at = CH * (p + a)
                    toep[level * 3 + b, p * CH : (p + 1) * CH, at : at + CH] = tap

    f32, bf16 = jnp.float32, jnp.bfloat16
    lane = lax.broadcasted_iota(jnp.int32, (CH, LANES), 1)
    column = lane + (c * COLS - SIDE)
    inside = jnp.logical_and(column >= 0, column < m * COLS)
    keep = jnp.where(inside, 1.0, 0.0)
    above = jnp.where(r > 0, 1.0, 0.0)
    below = jnp.where(r < n - 1, 1.0, 0.0)

    def taps(value, dilation):
        return [
            pltpu.roll(value, dilation, 1),
            value,
            pltpu.roll(value, LANES - dilation, 1),
        ]

    def masks(dilation):
        return [
            [part.astype(bf16) for part in taps(keep * edge, dilation)]
            for edge in (above, 1.0, below)
        ]

    def zone(row):
        return 0 if row < HALO else (1 if row < HALO + ROWS else 2)

    def row_band(slot_value, where):
        return jnp.broadcast_to(slot_value[:, where : where + 1], (CH, LANES)).astype(bf16)

    mine = own[0].astype(f32)
    for row in range(ROWS):
        xb[1, HALO + row] = row_band(mine, row)

    diagonal = lax.broadcasted_iota(jnp.int32, (CH, CH), 0) == lax.broadcasted_iota(
        jnp.int32, (CH, CH), 1
    )

    def level_bias(level):
        spread = jnp.where(diagonal, bias_ref[level : level + 1, :], 0.0)
        one = jnp.broadcast_to(jnp.sum(spread, axis=1, keepdims=True), (CH, LANES))
        one = jnp.concatenate([one, one], axis=1)
        return jnp.concatenate([one] * GROUP, axis=0)

    biases = [level_bias(level) for level in range(3)]
    tile_from = lax.broadcasted_iota(jnp.int32, (CH, SPAN * CH), 0)
    tile_to = lax.broadcasted_iota(jnp.int32, (CH, SPAN * CH), 1)
    tiler = jnp.where(tile_to % CH == tile_from, 1.0, 0.0).astype(bf16)
    head_rows = jnp.broadcast_to(head_ref[...].astype(f32), (8, CH)).astype(bf16)
    tiled = jnp.dot(head_rows, tiler, preferred_element_type=f32)
    line = lax.broadcasted_iota(jnp.int32, (8, SPAN * CH), 0)
    spot = lax.broadcasted_iota(jnp.int32, (8, SPAN * CH), 1)
    head = jnp.where(spot // CH == line, tiled, 0.0).astype(bf16)

    pl.when(r > 0)(lambda: copy(0, 0, r - 1, 0).wait_recv())
    pl.when(r < n - 1)(lambda: copy(0, 1, r + 1, 1).wait_recv())
    pl.when(jnp.logical_not(is_owner))(lambda: copy(1, 2, owner, 2).wait_recv())
    pl.when(jnp.logical_and(has_side, jnp.logical_not(is_side)))(
        lambda: copy(1, 3, side, 2).wait_recv()
    )

    col_own = land[2].astype(f32)
    col_side = land[3].astype(f32)
    low = jnp.where(lane >= SIDE, pltpu.roll(col_own, SIDE, 1), pltpu.roll(col_side, SIDE, 1))
    high = jnp.where(
        lane < LANES - SIDE,
        pltpu.roll(col_own, LANES - SIDE, 1),
        pltpu.roll(col_side, LANES - SIDE, 1),
    )
    cols = [part.astype(bf16) for part in taps(jnp.where(half == 0, low, high), DILATIONS[0])]
    kept = masks(DILATIONS[0])
    before = land[0].astype(f32)
    after = land[1].astype(f32)
    for row in range(TALL):
        if zone(row) == 0:
            one = row_band(before, LANES - HALO + row)
        elif zone(row) == 2:
            one = row_band(after, row - HALO - ROWS)
        else:
            one = xb[1, row]
        for tap in range(3):
            xa[tap, row] = (one + cols[tap]) * kept[zone(row)][tap]

    def window(ref, tap, start, dilation):
        return jnp.concatenate(
            [ref[tap, start + dilation * (q - 1)] for q in range(SPAN)], axis=0
        )

    refs = (xa, xb, xa)
    for level, dilation in enumerate(DILATIONS):
        source = refs[level]
        if level < 2:
            kept = masks(DILATIONS[level + 1])
        begun = starts(level)
        for left, right in zip(begun[0::2], begun[1::2]):
            total = None
            for tap in range(3):
                seen = jnp.concatenate(
                    [window(source, tap, left, dilation), window(source, tap, right, dilation)],
                    axis=1,
                )
                part = jnp.dot(toep[level * 3 + tap], seen, preferred_element_type=f32)
                total = part if total is None else total + part
            value = jnp.maximum(total + biases[level], 0.0)
            for half_at, start in enumerate((left, right)):
                for p in range(GROUP):
                    row = start + dilation * p
                    piece = value[
                        p * CH : (p + 1) * CH, half_at * LANES : (half_at + 1) * LANES
                    ]
                    if level == 2:
                        last[row - HALO] = piece.astype(bf16)
                        continue
                    for tap, moved in enumerate(taps(piece, DILATIONS[level + 1])):
                        refs[level + 1][tap, row] = moved.astype(bf16) * kept[zone(row)][tap]
    for at in range(0, ROWS, 16):
        seen = jnp.concatenate(
            [
                jnp.concatenate([last[at + first + q] for q in range(SPAN)], axis=0)
                for first in (0, SPAN)
            ],
            axis=1,
        )
        lines = jnp.dot(head, seen, preferred_element_type=f32)
        gathered[at : at + SPAN] = lines[:, :LANES]
        gathered[at + SPAN : at + 2 * SPAN] = lines[:, LANES:]
    out_ref[...] = gathered[...].T[SIDE : SIDE + COLS]
    pl.when(r > 0)(lambda: copy(0, 1, r - 1, 0).wait_send())
    pl.when(r < n - 1)(lambda: copy(0, 0, r + 1, 1).wait_send())
    pl.when(jnp.logical_or(is_owner, is_side))(finish)


def body(embeddings, row_weight, col_weight, conv_weights, conv_bias, head_weight):
    n = lax.axis_size("row")
    vmem = pl.BlockSpec(memory_space=pltpu.VMEM)
    contact = pl.pallas_call(
        contact_kernel,
        out_shape=jax.ShapeDtypeStruct((COLS, ROWS), jnp.float32),
        in_specs=[pl.BlockSpec(memory_space=pltpu.HBM)] * 6,
        out_specs=vmem,
        scratch_shapes=[
            pltpu.VMEM(embeddings.shape, jnp.bfloat16),
            pltpu.VMEM((2, CH, embeddings.shape[1]), jnp.bfloat16),
            pltpu.VMEM((3, 3, 3, CH, CH), jnp.bfloat16),
            pltpu.VMEM((3, CH), jnp.float32),
            pltpu.VMEM((1, CH), jnp.bfloat16),
            pltpu.VMEM((2, CH, LANES), jnp.bfloat16),
            pltpu.VMEM((4, CH, LANES), jnp.bfloat16),
            pltpu.VMEM((9, GROUP * CH, SPAN * CH), jnp.bfloat16),
            pltpu.VMEM((3, TALL, CH, LANES), jnp.bfloat16),
            pltpu.VMEM((3, TALL, CH, LANES), jnp.bfloat16),
            pltpu.VMEM((ROWS, CH, LANES), jnp.bfloat16),
            pltpu.VMEM((ROWS, LANES), jnp.float32),
            pltpu.SemaphoreType.DMA((6,)),
            pltpu.SemaphoreType.DMA((n + 1,)),
            pltpu.SemaphoreType.DMA((4,)),
        ],
        compiler_params=pltpu.CompilerParams(collective_id=0, has_side_effects=True),
        name="contact",
    )(
        embeddings,
        row_weight.T,
        col_weight.T,
        conv_weights.transpose(0, 3, 4, 1, 2),
        conv_bias,
        head_weight.reshape(1, CH),
    )
    return contact.T


def solution(mesh):
    return jax.shard_map(
        body,
        mesh=mesh,
        in_specs=(P("row", None), P(), P(), P(), P(), P()),
        out_specs=P("row", "col"),
        check_vma=False,
    )
```

```python
import jax
import jax.numpy as jnp
from jax import lax
from jax.experimental import pallas as pl
from jax.experimental.pallas import tpu as pltpu
from jax.sharding import PartitionSpec as P

CH = 32
ROWS = 128
COLS = 64
LANES = 128
HALO = 7
TALL = ROWS + 2 * HALO
GROUP = 6
SPAN = GROUP + 2
SIDE = 32
DILATIONS = (1, 2, 4)


def starts(level):
    dilation = DILATIONS[level]
    reach = sum(DILATIONS[: level + 1])
    first, last = reach, TALL - reach
    found = []
    for phase in range(dilation):
        rows = list(range(first + phase, last, dilation))
        at = 0
        while at < len(rows):
            at = min(at, len(rows) - GROUP)
            found.append(rows[at])
            at += GROUP
    return sorted(found)


def contact_kernel(
    emb_hbm,
    row_w_hbm,
    col_w_hbm,
    w_hbm,
    bias_hbm,
    head_hbm,
    out_ref,
    emb_ref,
    proj_ref,
    w_ref,
    bias_ref,
    head_ref,
    own,
    land,
    toep,
    band,
    xa,
    xb,
    last,
    gathered,
    load_sem,
    send_sem,
    recv_sem,
):
    loads = [
        pltpu.make_async_copy(source, target, load_sem.at[at])
        for at, (source, target) in enumerate(
            (
                (emb_hbm, emb_ref),
                (row_w_hbm, proj_ref.at[0]),
                (col_w_hbm, proj_ref.at[1]),
                (w_hbm, w_ref),
                (bias_hbm, bias_ref),
                (head_hbm, head_ref),
            )
        )
    ]
    for load in loads:
        load.start()

    n = lax.axis_size("row")
    m = lax.axis_size("col")
    r = lax.axis_index("row")
    c = lax.axis_index("col")
    half = c % 2
    owner = c // 2
    side = owner - 1 + 2 * half
    has_side = jnp.logical_and(side >= 0, side < n)
    is_owner = r == owner
    is_side = r == side
    barrier = pltpu.get_barrier_semaphore()

    def greet(row):
        pl.semaphore_signal(
            barrier, inc=1, device_id=(row, c), device_id_type=pl.DeviceIdType.MESH
        )

    pl.when(r > 0)(lambda: greet(r - 1))
    pl.when(r < n - 1)(lambda: greet(r + 1))
    pl.when(jnp.logical_not(is_owner))(lambda: greet(owner))
    pl.when(jnp.logical_and(has_side, jnp.logical_not(is_side)))(lambda: greet(side))

    for load in loads[:3]:
        load.wait()
    projected = lax.dot_general(
        jnp.concatenate([proj_ref[0], proj_ref[1]], axis=0),
        emb_ref[...],
        (((1,), (1,)), ((), ())),
        preferred_element_type=jnp.float32,
    ).astype(jnp.bfloat16)
    own[0] = projected[:CH]
    own[1] = projected[CH:]

    expected = (
        jnp.where(r > 0, 1, 0)
        + jnp.where(r < n - 1, 1, 0)
        + jnp.where(is_owner, n - 1, 0)
        + jnp.where(is_side, n - 1, 0)
    )
    pl.semaphore_wait(barrier, expected)

    def copy(source, slot, row, sem):
        return pltpu.make_async_remote_copy(
            src_ref=own.at[source],
            dst_ref=land.at[slot],
            send_sem=send_sem.at[sem],
            recv_sem=recv_sem.at[slot],
            device_id=(row, c),
            device_id_type=pl.DeviceIdType.MESH,
        )

    def broadcast(slot):
        order = sorted(range(1, n), key=lambda k: -min(k, n - k))
        for k in order:
            copy(1, slot, (r + k) % n, 1 + k).start()

    def finish():
        for k in range(1, n):
            copy(1, 2, (r + k) % n, 1 + k).wait_send()

    pl.when(is_owner)(lambda: broadcast(2))
    pl.when(is_side)(lambda: broadcast(3))
    pl.when(r > 0)(lambda: copy(0, 1, r - 1, 0).start())
    pl.when(r < n - 1)(lambda: copy(0, 0, r + 1, 1).start())

    def fill(slot, value):
        land[slot] = value

    blank = jnp.zeros((CH, LANES), jnp.bfloat16)
    pl.when(is_owner)(lambda: fill(2, own[1]))
    pl.when(is_side)(lambda: fill(3, own[1]))
    pl.when(jnp.logical_not(has_side))(lambda: fill(3, blank))
    pl.when(r == 0)(lambda: fill(0, blank))
    pl.when(r == n - 1)(lambda: fill(1, blank))

    toep[...] = jnp.zeros_like(toep)
    for load in loads[3:]:
        load.wait()
    for level in range(3):
        for b in range(3):
            for a in range(3):
                tap = w_ref[level, a, b]
                for p in range(GROUP):
                    at = CH * (p + a)
                    toep[level * 3 + b, p * CH : (p + 1) * CH, at : at + CH] = tap

    f32, bf16 = jnp.float32, jnp.bfloat16
    lane = lax.broadcasted_iota(jnp.int32, (CH, LANES), 1)
    column = lane + (c * COLS - SIDE)
    inside = jnp.logical_and(column >= 0, column < m * COLS)
    keep = jnp.where(inside, 1.0, 0.0)
    above = jnp.where(r > 0, 1.0, 0.0)
    below = jnp.where(r < n - 1, 1.0, 0.0)

    def taps(value, dilation):
        return [
            pltpu.roll(value, dilation, 1),
            value,
            pltpu.roll(value, LANES - dilation, 1),
        ]

    kept = [
        [part.astype(bf16) for part in taps(keep * edge, DILATIONS[0])]
        for edge in (above, 1.0, below)
    ]
    shut = -3.0e38

    def zone(row):
        return 0 if row < HALO else (1 if row < HALO + ROWS else 2)

    def row_band(slot_value, where):
        return jnp.broadcast_to(slot_value[:, where : where + 1], (CH, LANES)).astype(bf16)

    mine = own[0].astype(f32)
    for row in range(ROWS):
        one = row_band(mine, row)
        for tap in range(3):
            band[tap, row] = one * kept[1][tap]

    diagonal = lax.broadcasted_iota(jnp.int32, (CH, CH), 0) == lax.broadcasted_iota(
        jnp.int32, (CH, CH), 1
    )

    def level_bias(level):
        spread = jnp.where(diagonal, bias_ref[level : level + 1, :], 0.0)
        one = jnp.broadcast_to(jnp.sum(spread, axis=1, keepdims=True), (CH, LANES))
        if level == 2:
            return [one] * 3
        one = jnp.where(inside, one, shut)
        return [jnp.where(r > 0, one, shut), one, jnp.where(r < n - 1, one, shut)]

    biases = [level_bias(level) for level in range(3)]
    tile_from = lax.broadcasted_iota(jnp.int32, (CH, SPAN * CH), 0)
    tile_to = lax.broadcasted_iota(jnp.int32, (CH, SPAN * CH), 1)
    tiler = jnp.where(tile_to % CH == tile_from, 1.0, 0.0).astype(bf16)
    head_rows = jnp.broadcast_to(head_ref[...].astype(f32), (8, CH)).astype(bf16)
    tiled = jnp.dot(head_rows, tiler, preferred_element_type=f32)
    line = lax.broadcasted_iota(jnp.int32, (8, SPAN * CH), 0)
    spot = lax.broadcasted_iota(jnp.int32, (8, SPAN * CH), 1)
    head = jnp.where(spot // CH == line, tiled, 0.0).astype(bf16)

    pl.when(r > 0)(lambda: copy(0, 0, r - 1, 0).wait_recv())
    pl.when(r < n - 1)(lambda: copy(0, 1, r + 1, 1).wait_recv())
    pl.when(jnp.logical_not(is_owner))(lambda: copy(1, 2, owner, 2).wait_recv())
    pl.when(jnp.logical_and(has_side, jnp.logical_not(is_side)))(
        lambda: copy(1, 3, side, 2).wait_recv()
    )

    col_own = land[2].astype(f32)
    col_side = land[3].astype(f32)
    low = jnp.where(lane >= SIDE, pltpu.roll(col_own, SIDE, 1), pltpu.roll(col_side, SIDE, 1))
    high = jnp.where(
        lane < LANES - SIDE,
        pltpu.roll(col_own, LANES - SIDE, 1),
        pltpu.roll(col_side, LANES - SIDE, 1),
    )
    cols = [part.astype(bf16) for part in taps(jnp.where(half == 0, low, high), DILATIONS[0])]
    cols_kept = [cols[tap] * kept[1][tap] for tap in range(3)]
    before = land[0].astype(f32)
    after = land[1].astype(f32)
    for row in range(TALL):
        if zone(row) == 0:
            one = row_band(before, LANES - HALO + row)
        elif zone(row) == 2:
            one = row_band(after, row - HALO - ROWS)
        else:
            for tap in range(3):
                xa[tap, row] = band[tap, row - HALO] + cols_kept[tap]
            continue
        for tap in range(3):
            xa[tap, row] = (one + cols[tap]) * kept[zone(row)][tap]

    def window(ref, tap, start, dilation):
        return jnp.concatenate(
            [ref[tap, start + dilation * (q - 1)] for q in range(SPAN)], axis=0
        )

    def apply_head(at):
        seen = jnp.concatenate(
            [
                jnp.concatenate([last[at + first + q] for q in range(SPAN)], axis=0)
                for first in (0, SPAN)
            ],
            axis=1,
        )
        lines = jnp.dot(head, seen, preferred_element_type=f32)
        gathered[at : at + SPAN] = lines[:, :LANES]
        gathered[at + SPAN : at + 2 * SPAN] = lines[:, LANES:]

    refs = (xa, xb, xa)
    for level, dilation in enumerate(DILATIONS):
        source = refs[level]
        begun = starts(level)
        for left, right in zip(begun[0::2], begun[1::2]):
            total = None
            for tap in range(3):
                seen = jnp.concatenate(
                    [window(source, tap, left, dilation), window(source, tap, right, dilation)],
                    axis=1,
                )
                part = jnp.dot(toep[level * 3 + tap], seen, preferred_element_type=f32)
                total = part if total is None else total + part
            for half_at, start in enumerate((left, right)):
                for p in range(GROUP):
                    row = start + dilation * p
                    piece = total[
                        p * CH : (p + 1) * CH, half_at * LANES : (half_at + 1) * LANES
                    ]
                    piece = jnp.maximum(piece + biases[level][zone(row)], 0.0)
                    if level == 2:
                        last[row - HALO] = piece.astype(bf16)
                        continue
                    for tap, moved in enumerate(taps(piece, DILATIONS[level + 1])):
                        refs[level + 1][tap, row] = moved.astype(bf16)
    for at in range(0, ROWS, 2 * SPAN):
        apply_head(at)
    out_ref[...] = gathered[...].T[SIDE : SIDE + COLS]
    pl.when(r > 0)(lambda: copy(0, 1, r - 1, 0).wait_send())
    pl.when(r < n - 1)(lambda: copy(0, 0, r + 1, 1).wait_send())
    pl.when(jnp.logical_or(is_owner, is_side))(finish)


def body(embeddings, row_weight, col_weight, conv_weights, conv_bias, head_weight):
    n = lax.axis_size("row")
    vmem = pl.BlockSpec(memory_space=pltpu.VMEM)
    contact = pl.pallas_call(
        contact_kernel,
        out_shape=jax.ShapeDtypeStruct((COLS, ROWS), jnp.float32),
        in_specs=[pl.BlockSpec(memory_space=pltpu.HBM)] * 6,
        out_specs=vmem,
        scratch_shapes=[
            pltpu.VMEM(embeddings.shape, jnp.bfloat16),
            pltpu.VMEM((2, CH, embeddings.shape[1]), jnp.bfloat16),
            pltpu.VMEM((3, 3, 3, CH, CH), jnp.bfloat16),
            pltpu.VMEM((3, CH), jnp.float32),
            pltpu.VMEM((1, CH), jnp.bfloat16),
            pltpu.VMEM((2, CH, LANES), jnp.bfloat16),
            pltpu.VMEM((4, CH, LANES), jnp.bfloat16),
            pltpu.VMEM((9, GROUP * CH, SPAN * CH), jnp.bfloat16),
            pltpu.VMEM((3, ROWS, CH, LANES), jnp.bfloat16),
            pltpu.VMEM((3, TALL, CH, LANES), jnp.bfloat16),
            pltpu.VMEM((3, TALL, CH, LANES), jnp.bfloat16),
            pltpu.VMEM((ROWS, CH, LANES), jnp.bfloat16),
            pltpu.VMEM((ROWS, LANES), jnp.float32),
            pltpu.SemaphoreType.DMA((6,)),
            pltpu.SemaphoreType.DMA((n + 1,)),
            pltpu.SemaphoreType.DMA((4,)),
        ],
        compiler_params=pltpu.CompilerParams(collective_id=0, has_side_effects=True),
        name="contact",
    )(
        embeddings,
        row_weight.T,
        col_weight.T,
        conv_weights.transpose(0, 3, 4, 1, 2),
        conv_bias,
        head_weight.reshape(1, CH),
    )
    return contact.T


def solution(mesh):
    return jax.shard_map(
        body,
        mesh=mesh,
        in_specs=(P("row", None), P(), P(), P(), P(), P()),
        out_specs=P("row", "col"),
        check_vma=False,
    )
```

```python
import jax
import jax.numpy as jnp
from jax import lax
from jax.experimental import pallas as pl
from jax.experimental.pallas import tpu as pltpu
from jax.sharding import PartitionSpec as P

CH = 32
ROWS = 128
COLS = 64
LANES = 128
HALO = 7
TALL = ROWS + 2 * HALO
GROUP = 6
SPAN = GROUP + 2
SIDE = 32
DILATIONS = (1, 2, 4)


def starts(level):
    dilation = DILATIONS[level]
    reach = sum(DILATIONS[: level + 1])
    first, last = reach, TALL - reach
    found = []
    for phase in range(dilation):
        rows = list(range(first + phase, last, dilation))
        at = 0
        while at < len(rows):
            at = min(at, len(rows) - GROUP)
            found.append(rows[at])
            at += GROUP
    return sorted(found)


def contact_kernel(
    emb_hbm,
    row_w_hbm,
    col_w_hbm,
    w_hbm,
    bias_hbm,
    head_hbm,
    out_ref,
    emb_ref,
    proj_ref,
    w_ref,
    bias_ref,
    head_ref,
    own,
    land,
    toep,
    band,
    xa,
    xb,
    last,
    gathered,
    load_sem,
    send_sem,
    recv_sem,
):
    loads = [
        pltpu.make_async_copy(source, target, load_sem.at[at])
        for at, (source, target) in enumerate(
            (
                (emb_hbm, emb_ref),
                (row_w_hbm, proj_ref.at[0]),
                (col_w_hbm, proj_ref.at[1]),
                (w_hbm, w_ref),
                (bias_hbm, bias_ref),
                (head_hbm, head_ref),
            )
        )
    ]
    for load in loads:
        load.start()

    n = lax.axis_size("row")
    m = lax.axis_size("col")
    r = lax.axis_index("row")
    c = lax.axis_index("col")
    half = c % 2
    owner = c // 2
    side = owner - 1 + 2 * half
    has_side = jnp.logical_and(side >= 0, side < n)
    is_owner = r == owner
    is_side = r == side
    barrier = pltpu.get_barrier_semaphore()

    def greet(row):
        pl.semaphore_signal(
            barrier, inc=1, device_id=(row, c), device_id_type=pl.DeviceIdType.MESH
        )

    pl.when(r > 0)(lambda: greet(r - 1))
    pl.when(r < n - 1)(lambda: greet(r + 1))
    pl.when(jnp.logical_not(is_owner))(lambda: greet(owner))
    pl.when(jnp.logical_and(has_side, jnp.logical_not(is_side)))(lambda: greet(side))

    for load in loads[:3]:
        load.wait()
    projected = lax.dot_general(
        jnp.concatenate([proj_ref[0], proj_ref[1]], axis=0),
        emb_ref[...],
        (((1,), (1,)), ((), ())),
        preferred_element_type=jnp.float32,
    ).astype(jnp.bfloat16)
    own[0] = projected[:CH]
    own[1] = projected[CH:]

    expected = (
        jnp.where(r > 0, 1, 0)
        + jnp.where(r < n - 1, 1, 0)
        + jnp.where(is_owner, n - 1, 0)
        + jnp.where(is_side, n - 1, 0)
    )
    pl.semaphore_wait(barrier, expected)

    def copy(source, slot, row, sem):
        return pltpu.make_async_remote_copy(
            src_ref=own.at[source],
            dst_ref=land.at[slot],
            send_sem=send_sem.at[sem],
            recv_sem=recv_sem.at[slot],
            device_id=(row, c),
            device_id_type=pl.DeviceIdType.MESH,
        )

    def each_other(act):
        for row in range(n):
            pl.when(r != row)(lambda row=row: act(row))

    def broadcast(slot):
        each_other(lambda row: copy(1, slot, row, 2 + row).start())

    def finish():
        each_other(lambda row: copy(1, 2, row, 2 + row).wait_send())

    pl.when(is_owner)(lambda: broadcast(2))
    pl.when(is_side)(lambda: broadcast(3))
    pl.when(r > 0)(lambda: copy(0, 1, r - 1, 0).start())
    pl.when(r < n - 1)(lambda: copy(0, 0, r + 1, 1).start())

    def fill(slot, value):
        land[slot] = value

    blank = jnp.zeros((CH, LANES), jnp.bfloat16)
    pl.when(is_owner)(lambda: fill(2, own[1]))
    pl.when(is_side)(lambda: fill(3, own[1]))
    pl.when(jnp.logical_not(has_side))(lambda: fill(3, blank))
    pl.when(r == 0)(lambda: fill(0, blank))
    pl.when(r == n - 1)(lambda: fill(1, blank))

    toep[...] = jnp.zeros_like(toep)
    for load in loads[3:]:
        load.wait()
    for level in range(3):
        for b in range(3):
            for a in range(3):
                tap = w_ref[level, a, b]
                for p in range(GROUP):
                    at = CH * (p + a)
                    toep[level * 3 + b, p * CH : (p + 1) * CH, at : at + CH] = tap

    f32, bf16 = jnp.float32, jnp.bfloat16
    lane = lax.broadcasted_iota(jnp.int32, (CH, LANES), 1)
    column = lane + (c * COLS - SIDE)
    inside = jnp.logical_and(column >= 0, column < m * COLS)
    keep = jnp.where(inside, 1.0, 0.0)
    above = jnp.where(r > 0, 1.0, 0.0)
    below = jnp.where(r < n - 1, 1.0, 0.0)

    def taps(value, dilation):
        return [
            pltpu.roll(value, dilation, 1),
            value,
            pltpu.roll(value, LANES - dilation, 1),
        ]

    kept = [
        [part.astype(bf16) for part in taps(keep * edge, DILATIONS[0])]
        for edge in (above, 1.0, below)
    ]
    shut = -3.0e38

    def zone(row):
        return 0 if row < HALO else (1 if row < HALO + ROWS else 2)

    def row_band(slot_value, where):
        return jnp.broadcast_to(slot_value[:, where : where + 1], (CH, LANES)).astype(bf16)

    mine = own[0].astype(f32)
    for row in range(ROWS):
        one = row_band(mine, row)
        for tap in range(3):
            band[tap, row] = one * kept[1][tap]

    diagonal = lax.broadcasted_iota(jnp.int32, (CH, CH), 0) == lax.broadcasted_iota(
        jnp.int32, (CH, CH), 1
    )

    def level_bias(level):
        spread = jnp.where(diagonal, bias_ref[level : level + 1, :], 0.0)
        one = jnp.broadcast_to(jnp.sum(spread, axis=1, keepdims=True), (CH, LANES))
        if level == 2:
            return [one] * 3
        one = jnp.where(inside, one, shut)
        return [jnp.where(r > 0, one, shut), one, jnp.where(r < n - 1, one, shut)]

    biases = [level_bias(level) for level in range(3)]
    tile_from = lax.broadcasted_iota(jnp.int32, (CH, SPAN * CH), 0)
    tile_to = lax.broadcasted_iota(jnp.int32, (CH, SPAN * CH), 1)
    tiler = jnp.where(tile_to % CH == tile_from, 1.0, 0.0).astype(bf16)
    head_rows = jnp.broadcast_to(head_ref[...].astype(f32), (8, CH)).astype(bf16)
    tiled = jnp.dot(head_rows, tiler, preferred_element_type=f32)
    line = lax.broadcasted_iota(jnp.int32, (8, SPAN * CH), 0)
    spot = lax.broadcasted_iota(jnp.int32, (8, SPAN * CH), 1)
    head = jnp.where(spot // CH == line, tiled, 0.0).astype(bf16)

    pl.when(r > 0)(lambda: copy(0, 0, r - 1, 0).wait_recv())
    pl.when(r < n - 1)(lambda: copy(0, 1, r + 1, 1).wait_recv())
    pl.when(jnp.logical_not(is_owner))(lambda: copy(1, 2, owner, 2).wait_recv())
    pl.when(jnp.logical_and(has_side, jnp.logical_not(is_side)))(
        lambda: copy(1, 3, side, 2).wait_recv()
    )

    col_own = land[2].astype(f32)
    col_side = land[3].astype(f32)
    low = jnp.where(lane >= SIDE, pltpu.roll(col_own, SIDE, 1), pltpu.roll(col_side, SIDE, 1))
    high = jnp.where(
        lane < LANES - SIDE,
        pltpu.roll(col_own, LANES - SIDE, 1),
        pltpu.roll(col_side, LANES - SIDE, 1),
    )
    cols = [part.astype(bf16) for part in taps(jnp.where(half == 0, low, high), DILATIONS[0])]
    cols_kept = [cols[tap] * kept[1][tap] for tap in range(3)]
    before = land[0].astype(f32)
    after = land[1].astype(f32)
    for row in range(TALL):
        if zone(row) == 0:
            one = row_band(before, LANES - HALO + row)
        elif zone(row) == 2:
            one = row_band(after, row - HALO - ROWS)
        else:
            for tap in range(3):
                xa[tap, row] = band[tap, row - HALO] + cols_kept[tap]
            continue
        for tap in range(3):
            xa[tap, row] = (one + cols[tap]) * kept[zone(row)][tap]

    def window(ref, tap, start, dilation):
        return jnp.concatenate(
            [ref[tap, start + dilation * (q - 1)] for q in range(SPAN)], axis=0
        )

    def apply_head(at):
        seen = jnp.concatenate(
            [
                jnp.concatenate([last[at + first + q] for q in range(SPAN)], axis=0)
                for first in (0, SPAN)
            ],
            axis=1,
        )
        lines = jnp.dot(head, seen, preferred_element_type=f32)
        gathered[at : at + SPAN] = lines[:, :LANES]
        gathered[at + SPAN : at + 2 * SPAN] = lines[:, LANES:]

    refs = (xa, xb, xa)
    for level, dilation in enumerate(DILATIONS):
        source = refs[level]
        begun = starts(level)
        for left, right in zip(begun[0::2], begun[1::2]):
            total = None
            for tap in range(3):
                seen = jnp.concatenate(
                    [window(source, tap, left, dilation), window(source, tap, right, dilation)],
                    axis=1,
                )
                part = jnp.dot(toep[level * 3 + tap], seen, preferred_element_type=f32)
                total = part if total is None else total + part
            for half_at, start in enumerate((left, right)):
                for p in range(GROUP):
                    row = start + dilation * p
                    piece = total[
                        p * CH : (p + 1) * CH, half_at * LANES : (half_at + 1) * LANES
                    ]
                    piece = jnp.maximum(piece + biases[level][zone(row)], 0.0)
                    if level == 2:
                        last[row - HALO] = piece.astype(bf16)
                        continue
                    for tap, moved in enumerate(taps(piece, DILATIONS[level + 1])):
                        refs[level + 1][tap, row] = moved.astype(bf16)
    for at in range(0, ROWS, 2 * SPAN):
        apply_head(at)
    out_ref[...] = gathered[...].T[SIDE : SIDE + COLS]
    pl.when(r > 0)(lambda: copy(0, 1, r - 1, 0).wait_send())
    pl.when(r < n - 1)(lambda: copy(0, 0, r + 1, 1).wait_send())
    pl.when(jnp.logical_or(is_owner, is_side))(finish)


def body(embeddings, row_weight, col_weight, conv_weights, conv_bias, head_weight):
    n = lax.axis_size("row")
    vmem = pl.BlockSpec(memory_space=pltpu.VMEM)
    contact = pl.pallas_call(
        contact_kernel,
        out_shape=jax.ShapeDtypeStruct((COLS, ROWS), jnp.float32),
        in_specs=[pl.BlockSpec(memory_space=pltpu.HBM)] * 6,
        out_specs=vmem,
        scratch_shapes=[
            pltpu.VMEM(embeddings.shape, jnp.bfloat16),
            pltpu.VMEM((2, CH, embeddings.shape[1]), jnp.bfloat16),
            pltpu.VMEM((3, 3, 3, CH, CH), jnp.bfloat16),
            pltpu.VMEM((3, CH), jnp.float32),
            pltpu.VMEM((1, CH), jnp.bfloat16),
            pltpu.VMEM((2, CH, LANES), jnp.bfloat16),
            pltpu.VMEM((4, CH, LANES), jnp.bfloat16),
            pltpu.VMEM((9, GROUP * CH, SPAN * CH), jnp.bfloat16),
            pltpu.VMEM((3, ROWS, CH, LANES), jnp.bfloat16),
            pltpu.VMEM((3, TALL, CH, LANES), jnp.bfloat16),
            pltpu.VMEM((3, TALL, CH, LANES), jnp.bfloat16),
            pltpu.VMEM((ROWS, CH, LANES), jnp.bfloat16),
            pltpu.VMEM((ROWS, LANES), jnp.float32),
            pltpu.SemaphoreType.DMA((6,)),
            pltpu.SemaphoreType.DMA((n + 2,)),
            pltpu.SemaphoreType.DMA((4,)),
        ],
        compiler_params=pltpu.CompilerParams(
            collective_id=0, has_side_effects=True, vmem_limit_bytes=16 * 2**20
        ),
        name="contact",
    )(
        *[
            pltpu.with_memory_space_constraint(each, pltpu.HBM)
            for each in (
                embeddings,
                row_weight.T,
                col_weight.T,
                conv_weights.transpose(0, 3, 4, 1, 2),
                conv_bias,
                head_weight.reshape(1, CH),
            )
        ]
    )
    return contact.T


def solution(mesh):
    return jax.shard_map(
        body,
        mesh=mesh,
        in_specs=(P("row", None), P(), P(), P(), P(), P()),
        out_specs=P("row", "col"),
        check_vma=False,
    )
```

```python
import jax
import jax.numpy as jnp
from jax import lax
from jax.experimental import pallas as pl
from jax.experimental.pallas import tpu as pltpu
from jax.sharding import PartitionSpec as P

CH = 32
ROWS = 128
COLS = 64
LANES = 128
HALO = 7
TALL = ROWS + 2 * HALO
GROUP = 6
SPAN = GROUP + 2
SIDE = 32
PACKED = ROWS // 2
DILATIONS = (1, 2, 4)


def starts(level):
    dilation = DILATIONS[level]
    reach = sum(DILATIONS[: level + 1])
    first, last = reach, (TALL - reach if level < 2 else reach + PACKED)
    found = []
    for phase in range(dilation):
        rows = list(range(first + phase, last, dilation))
        at = 0
        while at < len(rows):
            at = min(at, len(rows) - GROUP)
            found.append(rows[at])
            at += GROUP
    return sorted(found)


def contact_kernel(
    emb_hbm,
    row_w_hbm,
    col_w_hbm,
    w_hbm,
    bias_hbm,
    head_hbm,
    out_ref,
    emb_ref,
    proj_ref,
    w_ref,
    bias_ref,
    head_ref,
    own,
    land,
    toep,
    band,
    xa,
    xb,
    xc,
    last,
    gathered,
    load_sem,
    send_sem,
    recv_sem,
):
    loads = [
        pltpu.make_async_copy(source, target, load_sem.at[at])
        for at, (source, target) in enumerate(
            (
                (emb_hbm, emb_ref),
                (row_w_hbm, proj_ref.at[0]),
                (col_w_hbm, proj_ref.at[1]),
                (w_hbm, w_ref),
                (bias_hbm, bias_ref),
                (head_hbm, head_ref),
            )
        )
    ]
    for load in loads:
        load.start()

    n = lax.axis_size("row")
    m = lax.axis_size("col")
    r = lax.axis_index("row")
    c = lax.axis_index("col")
    half = c % 2
    owner = c // 2
    side = owner - 1 + 2 * half
    has_side = jnp.logical_and(side >= 0, side < n)
    is_owner = r == owner
    is_side = r == side
    barrier = pltpu.get_barrier_semaphore()

    def greet(row):
        pl.semaphore_signal(
            barrier, inc=1, device_id=(row, c), device_id_type=pl.DeviceIdType.MESH
        )

    pl.when(r > 0)(lambda: greet(r - 1))
    pl.when(r < n - 1)(lambda: greet(r + 1))
    pl.when(jnp.logical_not(is_owner))(lambda: greet(owner))
    pl.when(jnp.logical_and(has_side, jnp.logical_not(is_side)))(lambda: greet(side))

    for load in loads[:3]:
        load.wait()
    projected = lax.dot_general(
        jnp.concatenate([proj_ref[0], proj_ref[1]], axis=0),
        emb_ref[...],
        (((1,), (1,)), ((), ())),
        preferred_element_type=jnp.float32,
    ).astype(jnp.bfloat16)
    own[0] = projected[:CH]
    own[1] = projected[CH:]

    expected = (
        jnp.where(r > 0, 1, 0)
        + jnp.where(r < n - 1, 1, 0)
        + jnp.where(is_owner, n - 1, 0)
        + jnp.where(is_side, n - 1, 0)
    )
    pl.semaphore_wait(barrier, expected)

    def copy(source, slot, row, sem):
        return pltpu.make_async_remote_copy(
            src_ref=own.at[source],
            dst_ref=land.at[slot],
            send_sem=send_sem.at[sem],
            recv_sem=recv_sem.at[slot],
            device_id=(row, c),
            device_id_type=pl.DeviceIdType.MESH,
        )

    def each_other(act):
        for row in range(n):
            pl.when(r != row)(lambda row=row: act(row))

    def broadcast(slot):
        each_other(lambda row: copy(1, slot, row, 2 + row).start())

    def finish():
        each_other(lambda row: copy(1, 2, row, 2 + row).wait_send())

    pl.when(is_owner)(lambda: broadcast(2))
    pl.when(is_side)(lambda: broadcast(3))
    pl.when(r > 0)(lambda: copy(0, 1, r - 1, 0).start())
    pl.when(r < n - 1)(lambda: copy(0, 0, r + 1, 1).start())

    def fill(slot, value):
        land[slot] = value

    blank = jnp.zeros((CH, LANES), jnp.bfloat16)
    pl.when(is_owner)(lambda: fill(2, own[1]))
    pl.when(is_side)(lambda: fill(3, own[1]))
    pl.when(jnp.logical_not(has_side))(lambda: fill(3, blank))
    pl.when(r == 0)(lambda: fill(0, blank))
    pl.when(r == n - 1)(lambda: fill(1, blank))

    toep[...] = jnp.zeros_like(toep)
    for load in loads[3:]:
        load.wait()
    for level in range(3):
        for b in range(3):
            for a in range(3):
                tap = w_ref[level, a, b]
                for p in range(GROUP):
                    at = CH * (p + a)
                    toep[level * 3 + b, p * CH : (p + 1) * CH, at : at + CH] = tap

    f32, bf16 = jnp.float32, jnp.bfloat16
    lane = lax.broadcasted_iota(jnp.int32, (CH, LANES), 1)
    column = lane + c * COLS - jnp.where(lane >= LANES - SIDE, LANES, 0)
    inside = jnp.logical_and(column >= 0, column < m * COLS)
    keep = jnp.where(inside, 1.0, 0.0)
    above = jnp.where(r > 0, 1.0, 0.0)
    below = jnp.where(r < n - 1, 1.0, 0.0)

    def taps(value, dilation):
        return [
            pltpu.roll(value, dilation, 1),
            value,
            pltpu.roll(value, LANES - dilation, 1),
        ]

    kept = [
        [part.astype(bf16) for part in taps(keep * edge, DILATIONS[0])]
        for edge in (above, 1.0, below)
    ]
    shut = -3.0e38

    def zone(row):
        return 0 if row < HALO else (1 if row < HALO + ROWS else 2)

    def row_band(slot_value, where):
        return jnp.broadcast_to(slot_value[:, where : where + 1], (CH, LANES)).astype(bf16)

    mine = own[0].astype(f32)
    for row in range(ROWS):
        one = row_band(mine, row)
        for tap in range(3):
            band[tap, row] = one * kept[1][tap]

    diagonal = lax.broadcasted_iota(jnp.int32, (CH, CH), 0) == lax.broadcasted_iota(
        jnp.int32, (CH, CH), 1
    )

    def level_bias(level):
        spread = jnp.where(diagonal, bias_ref[level : level + 1, :], 0.0)
        one = jnp.broadcast_to(jnp.sum(spread, axis=1, keepdims=True), (CH, LANES))
        if level == 2:
            return [one] * 3
        one = jnp.where(inside, one, shut)
        return [jnp.where(r > 0, one, shut), one, jnp.where(r < n - 1, one, shut)]

    biases = [level_bias(level) for level in range(3)]
    tile_from = lax.broadcasted_iota(jnp.int32, (CH, SPAN * CH), 0)
    tile_to = lax.broadcasted_iota(jnp.int32, (CH, SPAN * CH), 1)
    tiler = jnp.where(tile_to % CH == tile_from, 1.0, 0.0).astype(bf16)
    head_rows = jnp.broadcast_to(head_ref[...].astype(f32), (8, CH)).astype(bf16)
    tiled = jnp.dot(head_rows, tiler, preferred_element_type=f32)
    line = lax.broadcasted_iota(jnp.int32, (8, SPAN * CH), 0)
    spot = lax.broadcasted_iota(jnp.int32, (8, SPAN * CH), 1)
    head = jnp.where(spot // CH == line, tiled, 0.0).astype(bf16)

    pl.when(r > 0)(lambda: copy(0, 0, r - 1, 0).wait_recv())
    pl.when(r < n - 1)(lambda: copy(0, 1, r + 1, 1).wait_recv())
    pl.when(jnp.logical_not(is_owner))(lambda: copy(1, 2, owner, 2).wait_recv())
    pl.when(jnp.logical_and(has_side, jnp.logical_not(is_side)))(
        lambda: copy(1, 3, side, 2).wait_recv()
    )

    col_own = land[2].astype(f32)
    col_side = land[3].astype(f32)
    low = jnp.where(lane < LANES - SIDE, col_own, col_side)
    high = jnp.where(
        jnp.logical_and(lane >= COLS, lane < LANES - SIDE),
        pltpu.roll(col_side, COLS, 1),
        pltpu.roll(col_own, COLS, 1),
    )
    cols = [part.astype(bf16) for part in taps(jnp.where(half == 0, low, high), DILATIONS[0])]
    cols_kept = [cols[tap] * kept[1][tap] for tap in range(3)]
    before = land[0].astype(f32)
    after = land[1].astype(f32)
    for row in range(TALL):
        if zone(row) == 0:
            one = row_band(before, LANES - HALO + row)
        elif zone(row) == 2:
            one = row_band(after, row - HALO - ROWS)
        else:
            for tap in range(3):
                xa[tap, row] = band[tap, row - HALO] + cols_kept[tap]
            continue
        for tap in range(3):
            xa[tap, row] = (one + cols[tap]) * kept[zone(row)][tap]

    def window(ref, tap, start, dilation):
        return jnp.concatenate(
            [ref[tap, start + dilation * (q - 1)] for q in range(SPAN)], axis=0
        )

    def apply_head(at):
        seen = jnp.concatenate(
            [
                jnp.concatenate([last[at + first + q] for q in range(SPAN)], axis=0)
                for first in (0, SPAN)
            ],
            axis=1,
        )
        lines = jnp.dot(head, seen, preferred_element_type=f32)
        gathered[at : at + SPAN] = lines[:, :LANES]
        gathered[at + SPAN : at + 2 * SPAN] = lines[:, LANES:]

    def pack(row, piece):
        for tap in range(3):
            ahead = DILATIONS[2] * (tap - 1)
            if row < HALO + PACKED + DILATIONS[2]:
                moved = pltpu.roll(piece, (LANES - ahead) % LANES, 1) if ahead else piece
                moved = moved.astype(bf16)
                xc[tap, row, :, :COLS] = moved[:, :COLS]
            if row >= HALO + PACKED - DILATIONS[2]:
                moved = pltpu.roll(piece, COLS - ahead, 1).astype(bf16)
                xc[tap, row - PACKED, :, COLS:] = moved[:, COLS:]

    refs = (xa, xb, xc)
    for level, dilation in enumerate(DILATIONS):
        source = refs[level]
        begun = starts(level)
        for left, right in zip(begun[0::2], begun[1::2]):
            total = None
            for tap in range(3):
                seen = jnp.concatenate(
                    [window(source, tap, left, dilation), window(source, tap, right, dilation)],
                    axis=1,
                )
                part = jnp.dot(toep[level * 3 + tap], seen, preferred_element_type=f32)
                total = part if total is None else total + part
            for half_at, start in enumerate((left, right)):
                for p in range(GROUP):
                    row = start + dilation * p
                    piece = total[
                        p * CH : (p + 1) * CH, half_at * LANES : (half_at + 1) * LANES
                    ]
                    piece = jnp.maximum(piece + biases[level][zone(row)], 0.0)
                    if level == 2:
                        last[row - HALO] = piece.astype(bf16)
                        continue
                    if level == 1:
                        pack(row, piece)
                        continue
                    for tap, moved in enumerate(taps(piece, DILATIONS[level + 1])):
                        refs[level + 1][tap, row] = moved.astype(bf16)
    for at in range(0, PACKED, 2 * SPAN):
        apply_head(at)
    turned = gathered[...].T
    out_ref[:, :PACKED] = turned[:COLS]
    out_ref[:, PACKED:] = turned[COLS:]
    pl.when(r > 0)(lambda: copy(0, 1, r - 1, 0).wait_send())
    pl.when(r < n - 1)(lambda: copy(0, 0, r + 1, 1).wait_send())
    pl.when(jnp.logical_or(is_owner, is_side))(finish)


def body(embeddings, row_weight, col_weight, conv_weights, conv_bias, head_weight):
    n = lax.axis_size("row")
    vmem = pl.BlockSpec(memory_space=pltpu.VMEM)
    contact = pl.pallas_call(
        contact_kernel,
        out_shape=jax.ShapeDtypeStruct((COLS, ROWS), jnp.float32),
        in_specs=[pl.BlockSpec(memory_space=pltpu.HBM)] * 6,
        out_specs=vmem,
        scratch_shapes=[
            pltpu.VMEM(embeddings.shape, jnp.bfloat16),
            pltpu.VMEM((2, CH, embeddings.shape[1]), jnp.bfloat16),
            pltpu.VMEM((3, 3, 3, CH, CH), jnp.bfloat16),
            pltpu.VMEM((3, CH), jnp.float32),
            pltpu.VMEM((1, CH), jnp.bfloat16),
            pltpu.VMEM((2, CH, LANES), jnp.bfloat16),
            pltpu.VMEM((4, CH, LANES), jnp.bfloat16),
            pltpu.VMEM((9, GROUP * CH, SPAN * CH), jnp.bfloat16),
            pltpu.VMEM((3, ROWS, CH, LANES), jnp.bfloat16),
            pltpu.VMEM((3, TALL, CH, LANES), jnp.bfloat16),
            pltpu.VMEM((3, TALL, CH, LANES), jnp.bfloat16),
            pltpu.VMEM((3, HALO + PACKED + DILATIONS[2], CH, LANES), jnp.bfloat16),
            pltpu.VMEM((PACKED, CH, LANES), jnp.bfloat16),
            pltpu.VMEM((PACKED, LANES), jnp.float32),
            pltpu.SemaphoreType.DMA((6,)),
            pltpu.SemaphoreType.DMA((n + 2,)),
            pltpu.SemaphoreType.DMA((4,)),
        ],
        compiler_params=pltpu.CompilerParams(
            collective_id=0, has_side_effects=True, vmem_limit_bytes=16 * 2**20
        ),
        name="contact",
    )(
        *[
            pltpu.with_memory_space_constraint(each, pltpu.HBM)
            for each in (
                embeddings,
                row_weight.T,
                col_weight.T,
                conv_weights.transpose(0, 3, 4, 1, 2),
                conv_bias,
                head_weight.reshape(1, CH),
            )
        ]
    )
    return contact.T


def solution(mesh):
    return jax.shard_map(
        body,
        mesh=mesh,
        in_specs=(P("row", None), P(), P(), P(), P(), P()),
        out_specs=P("row", "col"),
        check_vma=False,
    )
```

```python
import jax
import jax.numpy as jnp
from jax import lax
from jax.experimental import pallas as pl
from jax.experimental.pallas import tpu as pltpu
from jax.sharding import PartitionSpec as P

CH = 32
ROWS = 128
COLS = 64
LANES = 128
HALO = 7
TALL = ROWS + 2 * HALO
GROUP = 6
SPAN = GROUP + 2
SIDE = 32
PACKED = ROWS // 2
DILATIONS = (1, 2, 4)


def starts(level):
    dilation = DILATIONS[level]
    reach = sum(DILATIONS[: level + 1])
    first, last = reach, (TALL - reach if level < 2 else reach + PACKED)
    found = []
    for phase in range(dilation):
        rows = list(range(first + phase, last, dilation))
        at = 0
        while at < len(rows):
            at = min(at, len(rows) - GROUP)
            found.append(rows[at])
            at += GROUP
    return sorted(found)


def contact_kernel(
    emb_hbm,
    row_w_hbm,
    col_w_hbm,
    w_hbm,
    bias_hbm,
    head_hbm,
    out_ref,
    emb_ref,
    proj_ref,
    w_ref,
    bias_ref,
    head_ref,
    own,
    land,
    toep,
    band,
    xa,
    xb,
    xc,
    last,
    gathered,
    load_sem,
    send_sem,
    recv_sem,
):
    loads = [
        pltpu.make_async_copy(source, target, load_sem.at[at])
        for at, (source, target) in enumerate(
            (
                (emb_hbm, emb_ref),
                (row_w_hbm, proj_ref.at[0]),
                (col_w_hbm, proj_ref.at[1]),
                (w_hbm, w_ref),
                (bias_hbm, bias_ref),
                (head_hbm, head_ref),
            )
        )
    ]
    for load in loads:
        load.start()

    n = lax.axis_size("row")
    m = lax.axis_size("col")
    r = lax.axis_index("row")
    c = lax.axis_index("col")
    half = c % 2
    owner = c // 2
    side = owner - 1 + 2 * half
    has_side = jnp.logical_and(side >= 0, side < n)
    is_owner = r == owner
    is_side = r == side
    low_rows = n // 2
    relay = jnp.where(c >= 2 * n - 3, n - 3, n - 1)
    is_relay = r == relay
    direct = jnp.logical_or(r < low_rows, is_relay)
    barrier = pltpu.get_barrier_semaphore()

    def greet(row):
        pl.semaphore_signal(
            barrier, inc=1, device_id=(row, c), device_id_type=pl.DeviceIdType.MESH
        )

    pl.when(r > 0)(lambda: greet(r - 1))
    pl.when(r < n - 1)(lambda: greet(r + 1))
    pl.when(jnp.logical_and(direct, jnp.logical_not(is_owner)))(lambda: greet(owner))
    pl.when(jnp.logical_and(jnp.logical_and(direct, has_side), jnp.logical_not(is_side)))(
        lambda: greet(side)
    )
    pl.when(jnp.logical_not(direct))(lambda: greet(relay))

    for load in loads[:3]:
        load.wait()
    projected = lax.dot_general(
        jnp.concatenate([proj_ref[0], proj_ref[1]], axis=0),
        emb_ref[...],
        (((1,), (1,)), ((), ())),
        preferred_element_type=jnp.float32,
    ).astype(jnp.bfloat16)
    own[0] = projected[:CH]
    own[1] = projected[CH:]

    expected = (
        jnp.where(r > 0, 1, 0)
        + jnp.where(r < n - 1, 1, 0)
        + jnp.where(jnp.logical_or(is_owner, is_side), low_rows + 1, 0)
        - jnp.where(jnp.logical_and(jnp.logical_or(is_owner, is_side), r < low_rows), 1, 0)
        + jnp.where(is_relay, n - low_rows - 1, 0)
    )
    pl.semaphore_wait(barrier, expected)

    def copy(source, slot, row, sem):
        return pltpu.make_async_remote_copy(
            src_ref=own.at[source],
            dst_ref=land.at[slot],
            send_sem=send_sem.at[sem],
            recv_sem=recv_sem.at[slot],
            device_id=(row, c),
            device_id_type=pl.DeviceIdType.MESH,
        )

    def each_direct(act):
        for row in range(low_rows):
            pl.when(r != row)(lambda row=row: act(row))
        act(relay)

    def each_high(source_row, act):
        for row in range(low_rows, n):
            pl.when(jnp.logical_and(row != relay, row != source_row))(lambda row=row: act(row))

    def broadcast(slot):
        each_direct(lambda row: copy(1, slot, row, 2 + row).start())

    def finish():
        each_direct(lambda row: copy(1, 2, row, 2 + row).wait_send())

    def forward(slot, row):
        return pltpu.make_async_remote_copy(
            src_ref=land.at[slot],
            dst_ref=land.at[slot],
            send_sem=send_sem.at[2 + row + (slot - 2) * n],
            recv_sem=recv_sem.at[slot],
            device_id=(row, c),
            device_id_type=pl.DeviceIdType.MESH,
        )

    pl.when(is_owner)(lambda: broadcast(2))
    pl.when(is_side)(lambda: broadcast(3))
    pl.when(r > 0)(lambda: copy(0, 1, r - 1, 0).start())
    pl.when(r < n - 1)(lambda: copy(0, 0, r + 1, 1).start())

    def fill(slot, value):
        land[slot] = value

    blank = jnp.zeros((CH, LANES), jnp.bfloat16)
    pl.when(is_owner)(lambda: fill(2, own[1]))
    pl.when(is_side)(lambda: fill(3, own[1]))
    pl.when(jnp.logical_not(has_side))(lambda: fill(3, blank))
    pl.when(r == 0)(lambda: fill(0, blank))
    pl.when(r == n - 1)(lambda: fill(1, blank))

    toep[...] = jnp.zeros_like(toep)
    for load in loads[3:]:
        load.wait()
    for level in range(3):
        for b in range(3):
            for a in range(3):
                tap = w_ref[level, a, b]
                for p in range(GROUP):
                    at = CH * (p + a)
                    toep[level * 3 + b, p * CH : (p + 1) * CH, at : at + CH] = tap

    f32, bf16 = jnp.float32, jnp.bfloat16
    lane = lax.broadcasted_iota(jnp.int32, (CH, LANES), 1)
    column = lane + c * COLS - jnp.where(lane >= LANES - SIDE, LANES, 0)
    inside = jnp.logical_and(column >= 0, column < m * COLS)
    keep = jnp.where(inside, 1.0, 0.0)
    above = jnp.where(r > 0, 1.0, 0.0)
    below = jnp.where(r < n - 1, 1.0, 0.0)

    def taps(value, dilation):
        return [
            pltpu.roll(value, dilation, 1),
            value,
            pltpu.roll(value, LANES - dilation, 1),
        ]

    kept = [
        [part.astype(bf16) for part in taps(keep * edge, DILATIONS[0])]
        for edge in (above, 1.0, below)
    ]
    shut = -3.0e38

    def zone(row):
        return 0 if row < HALO else (1 if row < HALO + ROWS else 2)

    def row_band(slot_value, where):
        return jnp.broadcast_to(slot_value[:, where : where + 1], (CH, LANES)).astype(bf16)

    mine = own[0].astype(f32)
    for row in range(ROWS):
        one = row_band(mine, row)
        for tap in range(3):
            band[tap, row] = one * kept[1][tap]

    diagonal = lax.broadcasted_iota(jnp.int32, (CH, CH), 0) == lax.broadcasted_iota(
        jnp.int32, (CH, CH), 1
    )

    def level_bias(level):
        spread = jnp.where(diagonal, bias_ref[level : level + 1, :], 0.0)
        one = jnp.broadcast_to(jnp.sum(spread, axis=1, keepdims=True), (CH, LANES))
        if level == 2:
            return [one] * 3
        one = jnp.where(inside, one, shut)
        return [jnp.where(r > 0, one, shut), one, jnp.where(r < n - 1, one, shut)]

    biases = [level_bias(level) for level in range(3)]
    tile_from = lax.broadcasted_iota(jnp.int32, (CH, SPAN * CH), 0)
    tile_to = lax.broadcasted_iota(jnp.int32, (CH, SPAN * CH), 1)
    tiler = jnp.where(tile_to % CH == tile_from, 1.0, 0.0).astype(bf16)
    head_rows = jnp.broadcast_to(head_ref[...].astype(f32), (8, CH)).astype(bf16)
    tiled = jnp.dot(head_rows, tiler, preferred_element_type=f32)
    line = lax.broadcasted_iota(jnp.int32, (8, SPAN * CH), 0)
    spot = lax.broadcasted_iota(jnp.int32, (8, SPAN * CH), 1)
    head = jnp.where(spot // CH == line, tiled, 0.0).astype(bf16)

    pl.when(r > 0)(lambda: copy(0, 0, r - 1, 0).wait_recv())
    pl.when(r < n - 1)(lambda: copy(0, 1, r + 1, 1).wait_recv())
    pl.when(jnp.logical_not(is_owner))(lambda: copy(1, 2, owner, 2).wait_recv())
    pl.when(jnp.logical_and(has_side, jnp.logical_not(is_side)))(
        lambda: copy(1, 3, side, 2).wait_recv()
    )
    pl.when(is_relay)(lambda: each_high(owner, lambda row: forward(2, row).start()))
    pl.when(jnp.logical_and(is_relay, has_side))(
        lambda: each_high(side, lambda row: forward(3, row).start())
    )

    col_own = land[2].astype(f32)
    col_side = land[3].astype(f32)
    low = jnp.where(lane < LANES - SIDE, col_own, col_side)
    high = jnp.where(
        jnp.logical_and(lane >= COLS, lane < LANES - SIDE),
        pltpu.roll(col_side, COLS, 1),
        pltpu.roll(col_own, COLS, 1),
    )
    cols = [part.astype(bf16) for part in taps(jnp.where(half == 0, low, high), DILATIONS[0])]
    cols_kept = [cols[tap] * kept[1][tap] for tap in range(3)]
    before = land[0].astype(f32)
    after = land[1].astype(f32)
    for row in range(TALL):
        if zone(row) == 0:
            one = row_band(before, LANES - HALO + row)
        elif zone(row) == 2:
            one = row_band(after, row - HALO - ROWS)
        else:
            for tap in range(3):
                xa[tap, row] = band[tap, row - HALO] + cols_kept[tap]
            continue
        for tap in range(3):
            xa[tap, row] = (one + cols[tap]) * kept[zone(row)][tap]

    def window(ref, tap, start, dilation):
        return jnp.concatenate(
            [ref[tap, start + dilation * (q - 1)] for q in range(SPAN)], axis=0
        )

    def apply_head(at):
        seen = jnp.concatenate(
            [
                jnp.concatenate([last[at + first + q] for q in range(SPAN)], axis=0)
                for first in (0, SPAN)
            ],
            axis=1,
        )
        lines = jnp.dot(head, seen, preferred_element_type=f32)
        gathered[at : at + SPAN] = lines[:, :LANES]
        gathered[at + SPAN : at + 2 * SPAN] = lines[:, LANES:]

    def pack(row, piece):
        for tap in range(3):
            ahead = DILATIONS[2] * (tap - 1)
            if row < HALO + PACKED + DILATIONS[2]:
                moved = pltpu.roll(piece, (LANES - ahead) % LANES, 1) if ahead else piece
                moved = moved.astype(bf16)
                xc[tap, row, :, :COLS] = moved[:, :COLS]
            if row >= HALO + PACKED - DILATIONS[2]:
                moved = pltpu.roll(piece, COLS - ahead, 1).astype(bf16)
                xc[tap, row - PACKED, :, COLS:] = moved[:, COLS:]

    refs = (xa, xb, xc)
    for level, dilation in enumerate(DILATIONS):
        source = refs[level]
        begun = starts(level)
        for left, right in zip(begun[0::2], begun[1::2]):
            total = None
            for tap in range(3):
                seen = jnp.concatenate(
                    [window(source, tap, left, dilation), window(source, tap, right, dilation)],
                    axis=1,
                )
                part = jnp.dot(toep[level * 3 + tap], seen, preferred_element_type=f32)
                total = part if total is None else total + part
            for half_at, start in enumerate((left, right)):
                for p in range(GROUP):
                    row = start + dilation * p
                    piece = total[
                        p * CH : (p + 1) * CH, half_at * LANES : (half_at + 1) * LANES
                    ]
                    piece = jnp.maximum(piece + biases[level][zone(row)], 0.0)
                    if level == 2:
                        last[row - HALO] = piece.astype(bf16)
                        continue
                    if level == 1:
                        pack(row, piece)
                        continue
                    for tap, moved in enumerate(taps(piece, DILATIONS[level + 1])):
                        refs[level + 1][tap, row] = moved.astype(bf16)
    for at in range(0, PACKED, 2 * SPAN):
        apply_head(at)
    turned = gathered[...].T
    out_ref[:, :PACKED] = turned[:COLS]
    out_ref[:, PACKED:] = turned[COLS:]
    pl.when(r > 0)(lambda: copy(0, 1, r - 1, 0).wait_send())
    pl.when(r < n - 1)(lambda: copy(0, 0, r + 1, 1).wait_send())
    pl.when(jnp.logical_or(is_owner, is_side))(finish)
    pl.when(is_relay)(lambda: each_high(owner, lambda row: forward(2, row).wait_send()))
    pl.when(jnp.logical_and(is_relay, has_side))(
        lambda: each_high(side, lambda row: forward(3, row).wait_send())
    )


def body(embeddings, row_weight, col_weight, conv_weights, conv_bias, head_weight):
    n = lax.axis_size("row")
    vmem = pl.BlockSpec(memory_space=pltpu.VMEM)
    contact = pl.pallas_call(
        contact_kernel,
        out_shape=jax.ShapeDtypeStruct((COLS, ROWS), jnp.float32),
        in_specs=[pl.BlockSpec(memory_space=pltpu.HBM)] * 6,
        out_specs=vmem,
        scratch_shapes=[
            pltpu.VMEM(embeddings.shape, jnp.bfloat16),
            pltpu.VMEM((2, CH, embeddings.shape[1]), jnp.bfloat16),
            pltpu.VMEM((3, 3, 3, CH, CH), jnp.bfloat16),
            pltpu.VMEM((3, CH), jnp.float32),
            pltpu.VMEM((1, CH), jnp.bfloat16),
            pltpu.VMEM((2, CH, LANES), jnp.bfloat16),
            pltpu.VMEM((4, CH, LANES), jnp.bfloat16),
            pltpu.VMEM((9, GROUP * CH, SPAN * CH), jnp.bfloat16),
            pltpu.VMEM((3, ROWS, CH, LANES), jnp.bfloat16),
            pltpu.VMEM((3, TALL, CH, LANES), jnp.bfloat16),
            pltpu.VMEM((3, TALL, CH, LANES), jnp.bfloat16),
            pltpu.VMEM((3, HALO + PACKED + DILATIONS[2], CH, LANES), jnp.bfloat16),
            pltpu.VMEM((PACKED, CH, LANES), jnp.bfloat16),
            pltpu.VMEM((PACKED, LANES), jnp.float32),
            pltpu.SemaphoreType.DMA((6,)),
            pltpu.SemaphoreType.DMA((2 * n + 2,)),
            pltpu.SemaphoreType.DMA((4,)),
        ],
        compiler_params=pltpu.CompilerParams(
            collective_id=0, has_side_effects=True, vmem_limit_bytes=16 * 2**20
        ),
        name="contact",
    )(
        *[
            pltpu.with_memory_space_constraint(each, pltpu.HBM)
            for each in (
                embeddings,
                row_weight.T,
                col_weight.T,
                conv_weights.transpose(0, 3, 4, 1, 2),
                conv_bias,
                head_weight.reshape(1, CH),
            )
        ]
    )
    return contact.T


def solution(mesh):
    return jax.shard_map(
        body,
        mesh=mesh,
        in_specs=(P("row", None), P(), P(), P(), P(), P()),
        out_specs=P("row", "col"),
        check_vma=False,
    )
```

```python
import jax
import jax.numpy as jnp
from jax import lax
from jax.experimental import pallas as pl
from jax.experimental.pallas import tpu as pltpu
from jax.sharding import PartitionSpec as P

CH = 32
ROWS = 128
COLS = 64
LANES = 128
HALO = 7
TALL = ROWS + 2 * HALO
GROUP = 6
SPAN = GROUP + 2
SIDE = 32
PACKED = ROWS // 2
DILATIONS = (1, 2, 4)


def starts(level):
    dilation = DILATIONS[level]
    reach = sum(DILATIONS[: level + 1])
    first, last = reach, (TALL - reach if level < 2 else reach + PACKED)
    found = []
    for phase in range(dilation):
        rows = list(range(first + phase, last, dilation))
        at = 0
        while at < len(rows):
            at = min(at, len(rows) - GROUP)
            found.append(rows[at])
            at += GROUP
    return sorted(found)


def contact_kernel(
    emb_hbm,
    row_w_hbm,
    col_w_hbm,
    w_hbm,
    bias_hbm,
    head_hbm,
    out_ref,
    emb_ref,
    proj_ref,
    w_ref,
    bias_ref,
    head_ref,
    own,
    land,
    toep,
    band,
    xa,
    xb,
    xc,
    last,
    gathered,
    load_sem,
    send_sem,
    recv_sem,
):
    loads = [
        pltpu.make_async_copy(source, target, load_sem.at[at])
        for at, (source, target) in enumerate(
            (
                (emb_hbm, emb_ref),
                (row_w_hbm, proj_ref.at[0]),
                (col_w_hbm, proj_ref.at[1]),
                (w_hbm, w_ref),
                (bias_hbm, bias_ref),
                (head_hbm, head_ref),
            )
        )
    ]
    for load in loads:
        load.start()

    n = lax.axis_size("row")
    m = lax.axis_size("col")
    r = lax.axis_index("row")
    c = lax.axis_index("col")
    half = c % 2
    owner = c // 2
    side = owner - 1 + 2 * half
    has_side = jnp.logical_and(side >= 0, side < n)
    is_owner = r == owner
    is_side = r == side
    low_rows = n // 2
    taken = jnp.logical_and(c >= n - 1, c <= n + 2)
    relay = jnp.where(taken, low_rows + 2, low_rows)
    is_relay = r == relay
    direct = jnp.logical_or(r < low_rows, is_relay)
    barrier = pltpu.get_barrier_semaphore()

    def greet(row):
        pl.semaphore_signal(
            barrier, inc=1, device_id=(row, c), device_id_type=pl.DeviceIdType.MESH
        )

    pl.when(r > 0)(lambda: greet(r - 1))
    pl.when(r < n - 1)(lambda: greet(r + 1))
    pl.when(jnp.logical_and(direct, jnp.logical_not(is_owner)))(lambda: greet(owner))
    pl.when(jnp.logical_and(jnp.logical_and(direct, has_side), jnp.logical_not(is_side)))(
        lambda: greet(side)
    )
    pl.when(jnp.logical_not(direct))(lambda: greet(relay))

    for load in loads[:3]:
        load.wait()
    projected = lax.dot_general(
        jnp.concatenate([proj_ref[0], proj_ref[1]], axis=0),
        emb_ref[...],
        (((1,), (1,)), ((), ())),
        preferred_element_type=jnp.float32,
    ).astype(jnp.bfloat16)
    own[0] = projected[:CH]
    own[1] = projected[CH:]

    expected = (
        jnp.where(r > 0, 1, 0)
        + jnp.where(r < n - 1, 1, 0)
        + jnp.where(jnp.logical_or(is_owner, is_side), low_rows + 1, 0)
        - jnp.where(jnp.logical_and(jnp.logical_or(is_owner, is_side), r < low_rows), 1, 0)
        + jnp.where(is_relay, n - low_rows - 1, 0)
    )
    pl.semaphore_wait(barrier, expected)

    def copy(source, slot, row, sem):
        return pltpu.make_async_remote_copy(
            src_ref=own.at[source],
            dst_ref=land.at[slot],
            send_sem=send_sem.at[sem],
            recv_sem=recv_sem.at[slot],
            device_id=(row, c),
            device_id_type=pl.DeviceIdType.MESH,
        )

    def each_direct(act):
        for row in range(low_rows):
            pl.when(r != row)(lambda row=row: act(row))
        act(relay)

    def each_high(source_row, act):
        for row in range(low_rows, n):
            pl.when(jnp.logical_and(row != relay, row != source_row))(lambda row=row: act(row))

    def broadcast(slot):
        each_direct(lambda row: copy(1, slot, row, 2 + row).start())

    def finish():
        each_direct(lambda row: copy(1, 2, row, 2 + row).wait_send())

    def forward(slot, row):
        return pltpu.make_async_remote_copy(
            src_ref=land.at[slot],
            dst_ref=land.at[slot],
            send_sem=send_sem.at[2 + row + (slot - 2) * n],
            recv_sem=recv_sem.at[slot],
            device_id=(row, c),
            device_id_type=pl.DeviceIdType.MESH,
        )

    pl.when(is_owner)(lambda: broadcast(2))
    pl.when(is_side)(lambda: broadcast(3))
    pl.when(r > 0)(lambda: copy(0, 1, r - 1, 0).start())
    pl.when(r < n - 1)(lambda: copy(0, 0, r + 1, 1).start())

    def fill(slot, value):
        land[slot] = value

    blank = jnp.zeros((CH, LANES), jnp.bfloat16)
    pl.when(is_owner)(lambda: fill(2, own[1]))
    pl.when(is_side)(lambda: fill(3, own[1]))
    pl.when(jnp.logical_not(has_side))(lambda: fill(3, blank))
    pl.when(r == 0)(lambda: fill(0, blank))
    pl.when(r == n - 1)(lambda: fill(1, blank))

    toep[...] = jnp.zeros_like(toep)
    for load in loads[3:]:
        load.wait()
    for level in range(3):
        for b in range(3):
            for a in range(3):
                tap = w_ref[level, a, b]
                for p in range(GROUP):
                    at = CH * (p + a)
                    toep[level * 3 + b, p * CH : (p + 1) * CH, at : at + CH] = tap

    f32, bf16 = jnp.float32, jnp.bfloat16
    lane = lax.broadcasted_iota(jnp.int32, (CH, LANES), 1)
    column = lane + c * COLS - jnp.where(lane >= LANES - SIDE, LANES, 0)
    inside = jnp.logical_and(column >= 0, column < m * COLS)
    keep = jnp.where(inside, 1.0, 0.0)
    above = jnp.where(r > 0, 1.0, 0.0)
    below = jnp.where(r < n - 1, 1.0, 0.0)

    def taps(value, dilation):
        return [
            pltpu.roll(value, dilation, 1),
            value,
            pltpu.roll(value, LANES - dilation, 1),
        ]

    kept = [
        [part.astype(bf16) for part in taps(keep * edge, DILATIONS[0])]
        for edge in (above, 1.0, below)
    ]
    shut = -3.0e38

    def zone(row):
        return 0 if row < HALO else (1 if row < HALO + ROWS else 2)

    def row_band(slot_value, where):
        return jnp.broadcast_to(slot_value[:, where : where + 1], (CH, LANES)).astype(bf16)

    mine = own[0].astype(f32)
    for row in range(ROWS):
        one = row_band(mine, row)
        for tap in range(3):
            band[tap, row] = one * kept[1][tap]

    diagonal = lax.broadcasted_iota(jnp.int32, (CH, CH), 0) == lax.broadcasted_iota(
        jnp.int32, (CH, CH), 1
    )

    def level_bias(level):
        spread = jnp.where(diagonal, bias_ref[level : level + 1, :], 0.0)
        one = jnp.broadcast_to(jnp.sum(spread, axis=1, keepdims=True), (CH, LANES))
        if level == 2:
            return [one] * 3
        one = jnp.where(inside, one, shut)
        return [jnp.where(r > 0, one, shut), one, jnp.where(r < n - 1, one, shut)]

    biases = [level_bias(level) for level in range(3)]
    tile_from = lax.broadcasted_iota(jnp.int32, (CH, SPAN * CH), 0)
    tile_to = lax.broadcasted_iota(jnp.int32, (CH, SPAN * CH), 1)
    tiler = jnp.where(tile_to % CH == tile_from, 1.0, 0.0).astype(bf16)
    head_rows = jnp.broadcast_to(head_ref[...].astype(f32), (8, CH)).astype(bf16)
    tiled = jnp.dot(head_rows, tiler, preferred_element_type=f32)
    line = lax.broadcasted_iota(jnp.int32, (8, SPAN * CH), 0)
    spot = lax.broadcasted_iota(jnp.int32, (8, SPAN * CH), 1)
    head = jnp.where(spot // CH == line, tiled, 0.0).astype(bf16)

    pl.when(r > 0)(lambda: copy(0, 0, r - 1, 0).wait_recv())
    pl.when(r < n - 1)(lambda: copy(0, 1, r + 1, 1).wait_recv())
    pl.when(jnp.logical_not(is_owner))(lambda: copy(1, 2, owner, 2).wait_recv())
    pl.when(jnp.logical_and(has_side, jnp.logical_not(is_side)))(
        lambda: copy(1, 3, side, 2).wait_recv()
    )
    pl.when(is_relay)(lambda: each_high(owner, lambda row: forward(2, row).start()))
    pl.when(jnp.logical_and(is_relay, has_side))(
        lambda: each_high(side, lambda row: forward(3, row).start())
    )

    col_own = land[2].astype(f32)
    col_side = land[3].astype(f32)
    low = jnp.where(lane < LANES - SIDE, col_own, col_side)
    high = jnp.where(
        jnp.logical_and(lane >= COLS, lane < LANES - SIDE),
        pltpu.roll(col_side, COLS, 1),
        pltpu.roll(col_own, COLS, 1),
    )
    cols = [part.astype(bf16) for part in taps(jnp.where(half == 0, low, high), DILATIONS[0])]
    cols_kept = [cols[tap] * kept[1][tap] for tap in range(3)]
    before = land[0].astype(f32)
    after = land[1].astype(f32)
    for row in range(TALL):
        if zone(row) == 0:
            one = row_band(before, LANES - HALO + row)
        elif zone(row) == 2:
            one = row_band(after, row - HALO - ROWS)
        else:
            for tap in range(3):
                xa[tap, row] = band[tap, row - HALO] + cols_kept[tap]
            continue
        for tap in range(3):
            xa[tap, row] = (one + cols[tap]) * kept[zone(row)][tap]

    def window(ref, tap, start, dilation):
        return jnp.concatenate(
            [ref[tap, start + dilation * (q - 1)] for q in range(SPAN)], axis=0
        )

    def apply_head(at):
        seen = jnp.concatenate(
            [
                jnp.concatenate([last[at + first + q] for q in range(SPAN)], axis=0)
                for first in (0, SPAN)
            ],
            axis=1,
        )
        lines = jnp.dot(head, seen, preferred_element_type=f32)
        gathered[at : at + SPAN] = lines[:, :LANES]
        gathered[at + SPAN : at + 2 * SPAN] = lines[:, LANES:]

    def pack(row, piece):
        for tap in range(3):
            ahead = DILATIONS[2] * (tap - 1)
            if row < HALO + PACKED + DILATIONS[2]:
                moved = pltpu.roll(piece, (LANES - ahead) % LANES, 1) if ahead else piece
                moved = moved.astype(bf16)
                xc[tap, row, :, :COLS] = moved[:, :COLS]
            if row >= HALO + PACKED - DILATIONS[2]:
                moved = pltpu.roll(piece, COLS - ahead, 1).astype(bf16)
                xc[tap, row - PACKED, :, COLS:] = moved[:, COLS:]

    refs = (xa, xb, xc)
    for level, dilation in enumerate(DILATIONS):
        source = refs[level]
        begun = starts(level)
        for left, right in zip(begun[0::2], begun[1::2]):
            total = None
            for tap in range(3):
                seen = jnp.concatenate(
                    [window(source, tap, left, dilation), window(source, tap, right, dilation)],
                    axis=1,
                )
                part = jnp.dot(toep[level * 3 + tap], seen, preferred_element_type=f32)
                total = part if total is None else total + part
            for half_at, start in enumerate((left, right)):
                for p in range(GROUP):
                    row = start + dilation * p
                    piece = total[
                        p * CH : (p + 1) * CH, half_at * LANES : (half_at + 1) * LANES
                    ]
                    piece = jnp.maximum(piece + biases[level][zone(row)], 0.0)
                    if level == 2:
                        last[row - HALO] = piece.astype(bf16)
                        continue
                    if level == 1:
                        pack(row, piece)
                        continue
                    for tap, moved in enumerate(taps(piece, DILATIONS[level + 1])):
                        refs[level + 1][tap, row] = moved.astype(bf16)
    for at in range(0, PACKED, 2 * SPAN):
        apply_head(at)
    turned = gathered[...].T
    out_ref[:, :PACKED] = turned[:COLS]
    out_ref[:, PACKED:] = turned[COLS:]
    pl.when(r > 0)(lambda: copy(0, 1, r - 1, 0).wait_send())
    pl.when(r < n - 1)(lambda: copy(0, 0, r + 1, 1).wait_send())
    pl.when(jnp.logical_or(is_owner, is_side))(finish)
    pl.when(is_relay)(lambda: each_high(owner, lambda row: forward(2, row).wait_send()))
    pl.when(jnp.logical_and(is_relay, has_side))(
        lambda: each_high(side, lambda row: forward(3, row).wait_send())
    )


def body(embeddings, row_weight, col_weight, conv_weights, conv_bias, head_weight):
    n = lax.axis_size("row")
    vmem = pl.BlockSpec(memory_space=pltpu.VMEM)
    contact = pl.pallas_call(
        contact_kernel,
        out_shape=jax.ShapeDtypeStruct((COLS, ROWS), jnp.float32),
        in_specs=[pl.BlockSpec(memory_space=pltpu.HBM)] * 6,
        out_specs=vmem,
        scratch_shapes=[
            pltpu.VMEM(embeddings.shape, jnp.bfloat16),
            pltpu.VMEM((2, CH, embeddings.shape[1]), jnp.bfloat16),
            pltpu.VMEM((3, 3, 3, CH, CH), jnp.bfloat16),
            pltpu.VMEM((3, CH), jnp.float32),
            pltpu.VMEM((1, CH), jnp.bfloat16),
            pltpu.VMEM((2, CH, LANES), jnp.bfloat16),
            pltpu.VMEM((4, CH, LANES), jnp.bfloat16),
            pltpu.VMEM((9, GROUP * CH, SPAN * CH), jnp.bfloat16),
            pltpu.VMEM((3, ROWS, CH, LANES), jnp.bfloat16),
            pltpu.VMEM((3, TALL, CH, LANES), jnp.bfloat16),
            pltpu.VMEM((3, TALL, CH, LANES), jnp.bfloat16),
            pltpu.VMEM((3, HALO + PACKED + DILATIONS[2], CH, LANES), jnp.bfloat16),
            pltpu.VMEM((PACKED, CH, LANES), jnp.bfloat16),
            pltpu.VMEM((PACKED, LANES), jnp.float32),
            pltpu.SemaphoreType.DMA((6,)),
            pltpu.SemaphoreType.DMA((2 * n + 2,)),
            pltpu.SemaphoreType.DMA((4,)),
        ],
        compiler_params=pltpu.CompilerParams(
            collective_id=0, has_side_effects=True, vmem_limit_bytes=16 * 2**20
        ),
        name="contact",
    )(
        *[
            pltpu.with_memory_space_constraint(each, pltpu.HBM)
            for each in (
                embeddings,
                row_weight.T,
                col_weight.T,
                conv_weights.transpose(0, 3, 4, 1, 2),
                conv_bias,
                head_weight.reshape(1, CH),
            )
        ]
    )
    return contact.T


def solution(mesh):
    return jax.shard_map(
        body,
        mesh=mesh,
        in_specs=(P("row", None), P(), P(), P(), P(), P()),
        out_specs=P("row", "col"),
        check_vma=False,
    )
```
